256 devices in a mesh: dp: 8 (over z_lo, x), fsdp: 32 (over y, z_hi, core).
Axes of the slice: x: 4, y: 4, z: 8 (z_hi: 4, z_lo: 2; z = z_hi * 2 + z_lo), core: 2. Of those that a mesh axis runs over, the one named last changes fastest.
Arguments:
- glu_out: bfloat16 [256, 768, 1536], P(('dp', 'fsdp')), may hold values from -6 to 6
- residual_in: bfloat16 [256, 768, 1536], P(('dp', 'fsdp')), may hold values from -6 to 6
- cotangent: bfloat16 [256, 768, 1536], P(('dp', 'fsdp')), may hold values from -6 to 6
- lengths: int32 [256], P(('dp', 'fsdp')), may hold values from 192 to 768, as said below
- conv_kernel: bfloat16 [5, 1536], P(None, 'fsdp'), may hold values from -2.5 to 2.5
- norm_gain: bfloat16 [1536], P('fsdp'), may hold values from 0.099609375 to 1.8984375
- norm_bias: bfloat16 [1536], P('fsdp'), may hold values from -3 to 3
- proj_weight: bfloat16 [1536, 1536], P('fsdp'), may hold values from -0.15625 to 0.15625
Outputs:
- block_out: bfloat16 [256, 768, 1536], P(('dp', 'fsdp'))
- glu_grad: bfloat16 [256, 768, 1536], P(('dp', 'fsdp'))
- proj_grad: float32 [1536, 1536], P('fsdp')
- kernel_grad: float32 [5, 1536], P(None, 'fsdp')
- norm_grads: float32 [2, 1536], P(None, 'fsdp')
The draws below stay inside these ranges and needn't reach their ends.
Inputs may be any that keep to these rules, and one draw needn't show every extreme that they name: `lengths`: lengths are drawn independently for each utterance; one utterance has all 768 frames valid and another has 192.
All inputs are finite; a program needn't handle non-finite values.
Results may differ from the reference program's by a relative error of at most 0.0029.
Values may be sent and summed in bfloat16 or wider, within the bound.
No kernel may reach another device: no remote copies, remote signals or barrier semaphores. Data moves between devices by JAX's collectives and lax.ppermute only.
A program may use at most 128 MiB of HBM per device.

```python
import jax
import jax.numpy as jnp
from jax import lax

D = 1536
TAPS = 5
FRAMES = 768
UTT_DEV = 1
UTTERANCES = 256
N_DP = 8
N_FSDP = 32


def draw_lengths(key, part):
    values = jax.random.randint(key, (UTTERANCES,), FRAMES // 4, FRAMES + 1).astype(jnp.int32)
    index = jnp.arange(UTTERANCES, dtype=jnp.int32)
    values = jnp.where(index == 0, jnp.int32(FRAMES), values)
    return jnp.where(index == 1, jnp.int32(FRAMES // 4), values)


def shard_levels(rng, shape, shards, least, largest):
    def one(position, parts):
        heights = jax.random.uniform(jax.random.fold_in(jax.random.fold_in(rng, 6), position), (parts,), jnp.float32, least / len(shards), largest / len(shards))
        return jnp.repeat(jnp.exp(heights), shape[position] // parts).reshape((-1,) + (1,) * (len(shape) - position - 1))

    level = one(*shards[0])
    for cut in shards[1:]:
        level = level * one(*cut)
    return level


def bell_draw(rng, extent, deviation, reach, pieces=(), kind=jnp.bfloat16):
    drawn = jax.random.normal(rng, extent, jnp.float32) * deviation
    if len(pieces) > 0:
        drawn = shard_levels(rng, extent, pieces, -0.22, 0.18) * drawn
    return jnp.clip(drawn, min=-reach, max=reach).astype(kind)


def setup_inputs(seed: int = 0) -> dict:
    streams_of = jax.random.split(jax.random.key(seed), 9)
    glu_out = bell_draw(streams_of[0], (UTTERANCES, FRAMES, D), 1.0, 6.0, ((0, 256),))
    residual_in = bell_draw(streams_of[1], (UTTERANCES, FRAMES, D), 1.0, 6.0, ((0, 256),))
    cotangent = bell_draw(streams_of[2], (UTTERANCES, FRAMES, D), 1.0, 6.0, ((0, 256),))
    lengths = draw_lengths(jax.random.fold_in(streams_of[8], 71), 0)
    conv_kernel = bell_draw(streams_of[4], (TAPS, D), TAPS ** -0.5, 2.5, ((1, 32),))
    norm_gain = jnp.clip(1.0 + 0.18 * jax.random.normal(streams_of[5], (D,), jnp.float32), 0.099609375, 1.8984375).astype(jnp.bfloat16)
    norm_bias = bell_draw(streams_of[6], (D,), 0.5, 3.0, ((0, 32),))
    proj_weight = bell_draw(streams_of[7], (D, D), D ** -0.5, 0.15625, ((0, 32),))
    return dict(glu_out=glu_out, residual_in=residual_in, cotangent=cotangent, lengths=lengths, conv_kernel=conv_kernel, norm_gain=norm_gain, norm_bias=norm_bias, proj_weight=proj_weight)


def one_device(glu, resid, cot, lens, kernel, gain, bias, weight):
    rows_count = glu.shape[0] * glu.shape[1]
    half = (TAPS - 1) // 2
    frame_ids = jnp.arange(glu.shape[1], dtype=jnp.int32)
    mask = (frame_ids[None, :] < lens[:, None]).astype(jnp.float32)[:, :, None]
    masked = glu.astype(jnp.float32) * mask
    padded = jnp.pad(masked, ((0, 0), (half, half), (0, 0)))
    conv = jnp.zeros_like(masked)
    for k in range(TAPS):
        conv = conv + kernel[k] * padded[:, k:k + glu.shape[1], :]
    mean_val = lax.optimization_barrier(jnp.mean(conv, axis=-1, keepdims=True))
    centred = conv - mean_val
    rstd = lax.rsqrt(lax.optimization_barrier(jnp.mean(centred * centred, axis=-1, keepdims=True)) + 1e-05)
    normed = centred * rstd
    pre = normed * gain + bias
    sig = jax.nn.sigmoid(pre)
    swished = (pre * sig).astype(jnp.bfloat16)
    flat = swished.reshape(rows_count, -1)
    proj = jnp.dot(flat, weight, preferred_element_type=jnp.float32).reshape(glu.shape)
    block_out = (resid.astype(jnp.float32) + mask * proj).astype(jnp.bfloat16)
    gout = (cot.astype(jnp.float32) * mask).astype(jnp.bfloat16)
    gflat = gout.reshape(rows_count, -1)
    term = jnp.dot(flat.T, gflat, preferred_element_type=jnp.float32)
    gswish = jnp.dot(gflat, weight.T, preferred_element_type=jnp.float32).reshape(glu.shape)
    gpre = gswish * sig * (1.0 + pre * (1.0 - sig))
    gain_term = lax.optimization_barrier(jnp.sum(gpre * normed, axis=(0, 1)))
    bias_term = lax.optimization_barrier(jnp.sum(gpre, axis=(0, 1)))
    gnorm = gpre * gain
    gconv = rstd * (gnorm - lax.optimization_barrier(jnp.mean(gnorm, axis=-1, keepdims=True)) - normed * lax.optimization_barrier(jnp.mean(gnorm * normed, axis=-1, keepdims=True)))
    kernel_terms = jnp.stack([lax.optimization_barrier(jnp.sum(gconv * padded[:, k:k + glu.shape[1], :], axis=(0, 1))) for k in range(TAPS)])
    gpad = jnp.pad(gconv, ((0, 0), (half, half), (0, 0)))
    gin = jnp.zeros_like(gconv)
    for k in range(TAPS):
        gin = gin + kernel[k] * gpad[:, TAPS - 1 - k:TAPS - 1 - k + glu.shape[1], :]
    glu_grad = (gin * mask).astype(jnp.bfloat16)
    small = jnp.concatenate([kernel_terms, gain_term[None], bias_term[None]], axis=0)
    return (block_out, glu_grad, term, small)

def reference(glu_out, residual_in, cotangent, lengths, conv_kernel, norm_gain, norm_bias, proj_weight):
    count = N_DP * N_FSDP
    kernel = conv_kernel.astype(jnp.float32)
    gain = norm_gain.astype(jnp.float32)
    bias = norm_bias.astype(jnp.float32)
    width = glu_out.shape[2]

    def step(carry, xs):
        glu, resid, cot, lens = xs
        out, grad, term, small = one_device(glu, resid, cot, lens, kernel, gain, bias, proj_weight)
        return ((carry[0] + term, carry[1] + small), (out, grad))
    shape4 = (count, UTT_DEV, FRAMES, width)
    xs = (glu_out.reshape(shape4), residual_in.reshape(shape4), cotangent.reshape(shape4), lengths.reshape(count, UTT_DEV))
    init = (jnp.zeros((width, width), jnp.float32), jnp.zeros((TAPS + 2, width), jnp.float32))
    sums, outs = lax.scan(step, init, xs)
    block_out = outs[0].reshape(glu_out.shape)
    glu_grad = outs[1].reshape(glu_out.shape)
    return (block_out, glu_grad, sums[0], sums[1][:TAPS], sums[1][TAPS:])
```

```python
import functools

import jax
import jax.numpy as jnp
from jax import lax
from jax.experimental import pallas as pl
from jax.experimental.pallas import tpu as pltpu
from jax.sharding import PartitionSpec as P

TAPS = 5
NX, NY, NZ = 4, 4, 4
F32, BF16 = jnp.float32, jnp.bfloat16
PAD = 8
VMEM_LIMIT = 60 * 1024 * 1024


def fsdp_move(value, y=0, z=0, core=0):
    perm = [(i, i ^ (y * 8 + z * 2 + core)) for i in range(32)]
    return lax.ppermute(value, "fsdp", perm)


def dp_move(value, x=0, low=0):
    perm = [(i, i ^ (low * 4 + x)) for i in range(8)]
    return lax.ppermute(value, "dp", perm)


def params(flops, read, exps=0):
    return dict(
        cost_estimate=pl.CostEstimate(flops=flops, bytes_accessed=read, transcendentals=exps),
    )


def compiler():
    return pltpu.CompilerParams(vmem_limit_bytes=VMEM_LIMIT)


def shifted(near, by, count):
    if by != 0:
        near = pltpu.roll(near, (-by) % near.shape[0], 0)
    return near[PAD : PAD + count]


def sds(shape, dtype):
    return jax.ShapeDtypeStruct(shape, dtype)


def whole(shape):
    return pl.BlockSpec(shape, lambda *_: (0,) * len(shape))


def forward_kernel(lens, par, glu, swished, normed, rstds, masked, *, rows, frames, chunk):
    step = pl.program_id(0)
    length = lens[0]
    width = glu.shape[1]

    @pl.when(step == 0)
    def _():
        masked[pl.ds(0, PAD), :] = jnp.zeros((PAD, width), F32)
        masked[pl.ds(PAD + frames, PAD), :] = jnp.zeros((PAD, width), F32)

        def fill(i, _):
            at = pl.multiple_of(i * 16, 16)
            ids = at + lax.broadcasted_iota(jnp.int32, (16, 1), 0)
            v = glu[pl.ds(at, 16), :].astype(F32)
            masked[pl.ds(pl.multiple_of(at + PAD, 8), 16), :] = jnp.where(ids < length, v, 0.0)
            return 0

        lax.fori_loop(0, frames // 16, fill, 0, unroll=4)

    def one(i, _):
        local = pl.multiple_of(i * chunk, chunk)
        base = step * rows + local
        near = masked[pl.ds(pl.multiple_of(base, 8), chunk + 2 * PAD), :]
        conv = par[0:1, :] * shifted(near, -2, chunk)
        for k in range(1, TAPS):
            conv = conv + par[k : k + 1, :] * shifted(near, k - 2, chunk)
        mean = jnp.sum(conv, axis=1, keepdims=True) * (1.0 / width)
        cent = conv - mean
        var = jnp.sum(cent * cent, axis=1, keepdims=True) * (1.0 / width)
        rstd = lax.rsqrt(var + 1e-05)
        norm = cent * rstd
        pre = norm * par[5:6, :] + par[6:7, :]
        sig = 0.5 * jnp.tanh(0.5 * pre) + 0.5
        ids = base + lax.broadcasted_iota(jnp.int32, (chunk, 1), 0)
        out = jnp.where(ids < length, pre * sig, 0.0)
        swished[pl.ds(local, chunk), :] = out.astype(BF16)
        normed[pl.ds(local, chunk), :] = norm
        rstds[pl.ds(local, chunk), :] = jnp.broadcast_to(rstd, (chunk, 128))
        return 0

    lax.fori_loop(0, rows // chunk, one, 0, unroll=2)


def forward(lens, par, glu, rows=128, chunk=16):
    frames, width = glu.shape
    block = lambda w: pl.BlockSpec((rows, w), lambda i, *_: (i, 0))
    return pl.pallas_call(
        functools.partial(forward_kernel, rows=rows, frames=frames, chunk=chunk),
        out_shape=(sds((frames, width), BF16), sds((frames, width), F32), sds((frames, 128), F32)),
        grid_spec=pltpu.PrefetchScalarGridSpec(
            num_scalar_prefetch=1,
            grid=(frames // rows,),
            in_specs=[whole((8, width)), whole((frames, width))],
            out_specs=(block(width), block(width), block(128)),
            scratch_shapes=[pltpu.VMEM((frames + 2 * PAD, width), F32)],
        ),
        compiler_params=compiler(),
        name="forward",
        **params(frames * width * 40, frames * width * 8, frames * width),
    )(lens, par, glu)


def outer_kernel(core, sw, cot, keep, send):
    res = lax.dot_general(
        sw[...], cot[...], (((0,), (0,)), ((), ())), preferred_element_type=F32
    )
    first = core[0] == 0
    for j in range(4):
        a = res[j * 96 : j * 96 + 48]
        b = res[j * 96 + 48 : j * 96 + 96]
        keep[j] = jnp.where(first, a, b)
        send[j] = jnp.where(first, b, a).astype(BF16)


def outer(core, sw, cot):
    frames, width = sw.shape
    return pl.pallas_call(
        outer_kernel,
        out_shape=(sds((16, 48, width), F32), sds((16, 48, width), BF16)),
        grid_spec=pltpu.PrefetchScalarGridSpec(
            num_scalar_prefetch=1,
            grid=(4,),
            in_specs=[
                pl.BlockSpec((frames, 384), lambda i, *_: (0, i)),
                whole((frames, width)),
            ],
            out_specs=(
                pl.BlockSpec((4, 48, width), lambda i, *_: (i, 0, 0)),
                pl.BlockSpec((4, 48, width), lambda i, *_: (i, 0, 0)),
            ),
        ),
        compiler_params=compiler(),
        name="outer",
        **params(2 * frames * width * width, 4 * frames * width + 6 * 768 * width),
    )(core, sw, cot)


def stage1_kernel(pos, keep, recv, a0, a1, a2, a3, b0, b1, b2, b3, tmp):
    j = pl.program_id(0)
    x = pos[1]
    for n, out in enumerate((a0, a1, a2, a3)):

        @pl.when(j == n)
        def _(out=out):
            out[...] = (keep[0, 0:2] + recv[0, 0:2].astype(F32)).astype(out.dtype)

    tmp[...] = keep[0, 2:4] + recv[0, 2:4].astype(F32)
    for n, out in enumerate((b0, b1, b2, b3)):
        at = pl.multiple_of((x ^ n) * 384, 128)
        out[0] = tmp[:, :, pl.ds(at, 384)].astype(out.dtype)


def stage1(pos, keep, recv):
    width = keep.shape[-1]
    keep = keep.reshape(4, 4, 48, width)
    recv = recv.reshape(4, 4, 48, width)
    src = pl.BlockSpec((1, 4, 48, width), lambda j, pos: (pos[0] ^ j, 0, 0, 0))
    a = whole((2, 48, width))
    b = pl.BlockSpec((1, 2, 48, 384), lambda j, pos: (pos[0] ^ j, 0, 0, 0))
    kinds = (F32, BF16, BF16, BF16)
    return pl.pallas_call(
        stage1_kernel,
        out_shape=tuple(sds((2, 48, width), t) for t in kinds) + tuple(sds((4, 2, 48, 384), t) for t in kinds),
        grid_spec=pltpu.PrefetchScalarGridSpec(
            num_scalar_prefetch=1,
            grid=(4,),
            in_specs=[src, src],
            out_specs=(a,) * 4 + (b,) * 4,
            scratch_shapes=[pltpu.VMEM((2, 48, width), F32)],
        ),
        compiler_params=compiler(),
        name="stage1",
        **params(768 * width, 768 * width * 9),
    )(pos, keep, recv)


def stage2_kernel(pos, a0, a1, a2, a3, b0, b1, b2, b3, *rest):
    outs, ta, tb = rest[:8], rest[8], rest[9]
    y, x = pos[0], pos[1]
    ta[...] = (a0[...] + a1[...].astype(F32)) + (a2[...].astype(F32) + a3[...].astype(F32))
    tb[...] = (b0[...] + b1[...].astype(F32)) + (b2[...].astype(F32) + b3[...].astype(F32))
    for n in range(4):
        at = pl.multiple_of((x ^ n) * 384, 128)
        outs[n][...] = ta[:, :, pl.ds(at, 384)]
        outs[4 + n][...] = tb[y ^ n]


def stage2(pos, a, b):
    width = a[0].shape[-1]
    return pl.pallas_call(
        stage2_kernel,
        out_shape=(sds((2, 48, 384), F32),) * 8,
        grid_spec=pltpu.PrefetchScalarGridSpec(
            num_scalar_prefetch=1,
            grid=(1,),
            in_specs=[whole((2, 48, width))] * 4 + [whole((4, 2, 48, 384))] * 4,
            out_specs=(whole((2, 48, 384)),) * 8,
            scratch_shapes=[pltpu.VMEM((2, 48, width), F32), pltpu.VMEM((4, 2, 48, 384), F32)],
        ),
        compiler_params=compiler(),
        name="stage2",
        **params(8 * 96 * width, 96 * width * 30),
    )(pos, *a, *b)


def stage3_kernel(pos, a0, a1, a2, a3, b0, b1, b2, b3, o0, o1, o2, o3, tmp):
    z = pos[2]
    tmp[0:2] = (a0[...] + a1[...]) + (a2[...] + a3[...])
    tmp[2:4] = (b0[...] + b1[...]) + (b2[...] + b3[...])
    for n, out in enumerate((o0, o1, o2, o3)):
        out[...] = tmp[z ^ n]


def stage3(pos, a, b):
    return pl.pallas_call(
        stage3_kernel,
        out_shape=(sds((48, 384), F32),) * 4,
        grid_spec=pltpu.PrefetchScalarGridSpec(
            num_scalar_prefetch=1,
            grid=(1,),
            in_specs=[whole((2, 48, 384))] * 8,
            out_specs=(whole((48, 384)),) * 4,
            scratch_shapes=[pltpu.VMEM((4, 48, 384), F32)],
        ),
        compiler_params=compiler(),
        name="stage3",
        **params(8 * 96 * 384, 96 * 384 * 48),
    )(pos, *a, *b)


def join_kernel(pos, v0, v1, v2, v3, out):
    x = pos[1]
    for n, v in enumerate((v0, v1, v2, v3)):
        at = pl.multiple_of((x ^ n) * 384, 128)
        out[:, pl.ds(at, 384)] = v[...]


def join(pos, parts):
    return pl.pallas_call(
        join_kernel,
        out_shape=sds((48, 1536), F32),
        grid_spec=pltpu.PrefetchScalarGridSpec(
            num_scalar_prefetch=1,
            grid=(1,),
            in_specs=[whole((48, 384))] * 4,
            out_specs=whole((48, 1536)),
        ),
        compiler_params=compiler(),
        name="join",
        **params(0, 48 * 1536 * 8),
    )(pos, *parts)


def fetch_weight(pos, pieces, buf, sem):
    y, z, core = pos[0], pos[2], pos[3]
    copies = []
    for n, piece in enumerate(pieces):
        dc, dy = n // 4, n % 4
        for dz in range(4):
            index = ((y ^ dy) * 4 + (z ^ dz)) * 2 + (core ^ dc)
            at = pl.multiple_of(index * 48, 48)
            copies.append(
                pltpu.make_async_copy(
                    piece.at[pl.ds(dz * 48, 48), :], buf.at[pl.ds(at, 48), :], sem.at[n * 4 + dz]
                )
            )
    for c in copies:
        c.start()
    for c in copies:
        c.wait()


def project_kernel(pos, *refs):
    pieces, (sw, res, out, buf, sem) = refs[:8], refs[8:]

    @pl.when(pl.program_id(0) == 0)
    def _():
        fetch_weight(pos, pieces, buf, sem)

    prod = jnp.dot(sw[...], buf[...], preferred_element_type=F32)
    out[...] = (res[...].astype(F32) + prod).astype(BF16)


def project(pos, pieces, sw, res, rows=128):
    frames, width = sw.shape
    block = pl.BlockSpec((rows, width), lambda i, *_: (i, 0))
    return pl.pallas_call(
        project_kernel,
        out_shape=sds((frames, width), BF16),
        grid_spec=pltpu.PrefetchScalarGridSpec(
            num_scalar_prefetch=1,
            grid=(frames // rows,),
            in_specs=[pl.BlockSpec(memory_space=pl.ANY)] * 8 + [block, block],
            out_specs=block,
            scratch_shapes=[pltpu.VMEM((width, width), BF16), pltpu.SemaphoreType.DMA((32,))],
        ),
        compiler_params=compiler(),
        name="project",
        **params(2 * frames * width * width, 6 * frames * width + 2 * width * width),
    )(pos, *pieces, sw, res)


def backward_kernel(pos, *refs, rows, chunk):
    pieces = refs[:8]
    par, cot, nrm, rst, gconv, sums, buf, sem, grad = refs[8:]
    step = pl.program_id(0)
    width = cot.shape[1]
    length = pos[4]

    @pl.when(step == 0)
    def _():
        fetch_weight(pos, pieces, buf, sem)
        sums[...] = jnp.zeros_like(sums)

    grad[...] = lax.dot_general(
        cot[...], buf[...], (((1,), (1,)), ((), ())), preferred_element_type=F32
    )

    def one(i, _):
        at = pl.multiple_of(i * chunk, chunk)
        gain = par[5:6, :]
        norm = nrm[pl.ds(at, chunk), :]
        pre = norm * gain + par[6:7, :]
        sig = 0.5 * jnp.tanh(0.5 * pre) + 0.5
        ids = step * rows + at + lax.broadcasted_iota(jnp.int32, (chunk, 1), 0)
        gs = jnp.where(ids < length, grad[pl.ds(at, chunk), :], 0.0)
        gpre = gs * (sig * (1.0 + pre * (1.0 - sig)))
        gn = gpre * norm
        for h in range(chunk // 8):
            sums[0] += gn[h * 8 : h * 8 + 8]
            sums[1] += gpre[h * 8 : h * 8 + 8]
        gnorm = gpre * gain
        m1 = jnp.sum(gnorm, axis=1, keepdims=True) * (1.0 / width)
        m2 = jnp.sum(gnorm * norm, axis=1, keepdims=True) * (1.0 / width)
        gconv[pl.ds(at, chunk), :] = rst[pl.ds(at, chunk), 0:1] * (gnorm - m1 - norm * m2)
        return 0

    lax.fori_loop(0, rows // chunk, one, 0, unroll=2)


def backward(pos, pieces, par, cot, nrm, rst, rows=128, chunk=16):
    frames, width = cot.shape
    block = lambda w: pl.BlockSpec((rows, w), lambda i, *_: (i, 0))
    return pl.pallas_call(
        functools.partial(backward_kernel, rows=rows, chunk=chunk),
        out_shape=(sds((frames, width), F32), sds((2, 8, width), F32)),
        grid_spec=pltpu.PrefetchScalarGridSpec(
            num_scalar_prefetch=1,
            grid=(frames // rows,),
            in_specs=[pl.BlockSpec(memory_space=pl.ANY)] * 8
            + [whole((8, width)), block(width), block(width), block(128)],
            out_specs=(block(width), whole((2, 8, width))),
            scratch_shapes=[
                pltpu.VMEM((width, width), BF16),
                pltpu.SemaphoreType.DMA((32,)),
                pltpu.VMEM((rows, width), F32),
            ],
        ),
        compiler_params=compiler(),
        name="backward",
        **params(2 * frames * width * width, 10 * frames * width + 2 * width * width, frames * width),
    )(pos, *pieces, par, cot, nrm, rst)


def taps_kernel(pos, par, glu, gconv, out, sums, pad, *, rows, frames, chunk):
    step = pl.program_id(0)
    width = glu.shape[1]
    length = pos[4]

    @pl.when(step == 0)
    def _():
        sums[...] = jnp.zeros_like(sums)
        pad[pl.ds(0, PAD), :] = jnp.zeros((PAD, width), F32)
        pad[pl.ds(PAD + frames, PAD), :] = jnp.zeros((PAD, width), F32)

    @pl.when(step < frames // rows)
    def _():
        pad[pl.ds(pl.multiple_of(PAD + step * rows, 8), rows), :] = gconv[...]

    @pl.when(step > 0)
    def _():
        def one(i, _):
            at = pl.multiple_of(i * chunk, chunk)
            base = (step - 1) * rows + at
            ids = base + lax.broadcasted_iota(jnp.int32, (chunk, 1), 0)
            live = ids < length
            mk = jnp.where(live, glu[pl.ds(at, chunk), :].astype(F32), 0.0)
            near = pad[pl.ds(pl.multiple_of(base, 8), chunk + 2 * PAD), :]
            acc = None
            for k in range(TAPS):
                g = shifted(near, 2 - k, chunk)
                term = par[k : k + 1, :] * g
                acc = term if acc is None else acc + term
                p = mk * g
                for h in range(chunk // 8):
                    sums[k] += p[h * 8 : h * 8 + 8]
            out[pl.ds(at, chunk), :] = jnp.where(live, acc, 0.0).astype(BF16)
            return 0

        lax.fori_loop(0, rows // chunk, one, 0, unroll=2)


def taps(pos, par, glu, gconv, rows=128, chunk=16):
    frames, width = glu.shape
    last = frames // rows - 1
    late = pl.BlockSpec((rows, width), lambda i, *_: (jnp.maximum(i - 1, 0), 0))
    return pl.pallas_call(
        functools.partial(taps_kernel, rows=rows, frames=frames, chunk=chunk),
        out_shape=(sds((frames, width), BF16), sds((TAPS, 8, width), F32)),
        grid_spec=pltpu.PrefetchScalarGridSpec(
            num_scalar_prefetch=1,
            grid=(frames // rows + 1,),
            in_specs=[
                whole((8, width)),
                late,
                pl.BlockSpec((rows, width), lambda i, *_: (jnp.minimum(i, last), 0)),
            ],
            out_specs=(late, whole((TAPS, 8, width))),
            scratch_shapes=[pltpu.VMEM((frames + 2 * PAD, width), F32)],
        ),
        compiler_params=compiler(),
        name="taps",
        **params(frames * width * 20, 8 * frames * width),
    )(pos, par, glu, gconv)


def local(glu_out, residual_in, cotangent, lengths, conv_kernel, norm_gain, norm_bias, proj_weight):
    _, frames, width = glu_out.shape
    glu, res, cot = glu_out[0], residual_in[0], cotangent[0]
    f, d = lax.axis_index("fsdp"), lax.axis_index("dp")
    core, z, y = f % 2, (f // 2) % 4, f // 8
    x = d % 4
    pos = jnp.stack([y, x, z, core, lengths[0]]).astype(jnp.int32)

    own = jnp.concatenate([conv_kernel, norm_gain[None], norm_bias[None]], axis=0)
    own = jnp.pad(own, ((0, 1), (0, 0)))
    par = lax.dynamic_update_slice(jnp.zeros((8, width), BF16), own, (0, f * 48))
    par = par + fsdp_move(par, core=1)
    par = par + fsdp_move(par, y=1) + fsdp_move(par, y=2) + fsdp_move(par, y=3)
    par = par + fsdp_move(par, z=1) + fsdp_move(par, z=2) + fsdp_move(par, z=3)
    par = par.astype(F32)

    block = jnp.concatenate([proj_weight] + [fsdp_move(proj_weight, z=k) for k in (1, 2, 3)], axis=0)
    near = [block] + [fsdp_move(block, y=k) for k in (1, 2, 3)]
    pieces = near + [fsdp_move(p, core=1) for p in near]

    swished, normed, rstd = forward(lengths, par, glu)
    keep, send = outer(core[None].astype(jnp.int32), swished, cot)
    recv = fsdp_move(send, core=1)

    s = stage1(pos, keep, recv)
    a = (s[0],) + tuple(fsdp_move(s[k], y=k) for k in (1, 2, 3))
    b = (s[4],) + tuple(dp_move(s[4 + k], x=k) for k in (1, 2, 3))
    s = stage2(pos, a, b)
    a = (s[0],) + tuple(dp_move(s[k], x=k) for k in (1, 2, 3))
    b = (s[4],) + tuple(fsdp_move(s[4 + k], y=k) for k in (1, 2, 3))
    s = stage3(pos, a, b)
    v = (s[0] + fsdp_move(s[1], z=1)) + (fsdp_move(s[2], z=2) + fsdp_move(s[3], z=3))
    v = v + dp_move(v, low=1)
    proj_grad = join(pos, [v] + [dp_move(v, x=k) for k in (1, 2, 3)])

    gconv, sums = backward(pos, pieces, par, cot, normed, rstd)
    glu_grad, tap_sums = taps(pos, par, glu, gconv)
    block_out = project(pos, pieces, swished, res)

    small = jnp.concatenate([tap_sums, sums, jnp.zeros((1, 8, width), F32)], axis=0).sum(axis=1)
    small = small + fsdp_move(small, core=1)
    small = (small + fsdp_move(small, y=1)) + (fsdp_move(small, y=2) + fsdp_move(small, y=3))
    small = (small + fsdp_move(small, z=1)) + (fsdp_move(small, z=2) + fsdp_move(small, z=3))
    small = lax.dynamic_slice(small, (0, f * 48), (8, 48))
    small = (small + dp_move(small, x=1)) + (dp_move(small, x=2) + dp_move(small, x=3))
    small = small + dp_move(small, low=1)
    return (block_out[None], glu_grad[None], proj_grad, small[:TAPS], small[TAPS : TAPS + 2])


def solution(mesh):
    rows = P(("dp", "fsdp"), None, None)
    return jax.shard_map(
        local,
        mesh=mesh,
        in_specs=(rows, rows, rows, P(("dp", "fsdp")), P(None, "fsdp"), P("fsdp"), P("fsdp"), P("fsdp", None)),
        out_specs=(rows, rows, P("fsdp", None), P(None, "fsdp"), P(None, "fsdp")),
        check_vma=False,
    )
```

```python
import functools

import jax
import jax.numpy as jnp
from jax import lax
from jax.experimental import pallas as pl
from jax.experimental.pallas import tpu as pltpu
from jax.sharding import PartitionSpec as P

TAPS = 5
NX, NY, NZ = 4, 4, 4
F32, BF16 = jnp.float32, jnp.bfloat16
PAD = 8
HBM = pl.BlockSpec(memory_space=pl.ANY)
VMEM_LIMIT = 60 * 1024 * 1024


def fsdp_move(value, y=0, z=0, core=0):
    perm = [(i, i ^ (y * 8 + z * 2 + core)) for i in range(32)]
    return lax.ppermute(value, "fsdp", perm)


def dp_move(value, x=0, low=0):
    perm = [(i, i ^ (low * 4 + x)) for i in range(8)]
    return lax.ppermute(value, "dp", perm)


def params(micros):
    return dict(
        cost_estimate=pl.CostEstimate(flops=0, bytes_accessed=int(micros * 3.6e6), transcendentals=0),
    )


def compiler():
    return pltpu.CompilerParams(vmem_limit_bytes=VMEM_LIMIT)


def shifted(near, by, count):
    if by != 0:
        near = pltpu.roll(near, (-by) % near.shape[0], 0)
    return near[PAD : PAD + count]


def sds(shape, dtype):
    return jax.ShapeDtypeStruct(shape, dtype)


def whole(shape):
    return pl.BlockSpec(shape, lambda *_: (0,) * len(shape))


def forward_kernel(lens, par, glu, swished, normed, rstds, masked, *, rows, frames, chunk, unroll):
    step = pl.program_id(0)
    length = lens[0]
    width = glu.shape[1]

    @pl.when(step == 0)
    def _():
        masked[pl.ds(0, PAD), :] = jnp.zeros((PAD, width), F32)
        masked[pl.ds(PAD + frames, PAD), :] = jnp.zeros((PAD, width), F32)

        def fill(i, _):
            at = pl.multiple_of(i * 16, 16)
            ids = at + lax.broadcasted_iota(jnp.int32, (16, 1), 0)
            v = glu[pl.ds(at, 16), :].astype(F32)
            masked[pl.ds(pl.multiple_of(at + PAD, 8), 16), :] = jnp.where(ids < length, v, 0.0)
            return 0

        lax.fori_loop(0, frames // 16, fill, 0, unroll=4)

    def one(i, _):
        local = pl.multiple_of(i * chunk, chunk)
        base = step * rows + local
        near = masked[pl.ds(pl.multiple_of(base, 8), chunk + 2 * PAD), :]
        conv = par[0:1, :] * shifted(near, -2, chunk)
        for k in range(1, TAPS):
            conv = conv + par[k : k + 1, :] * shifted(near, k - 2, chunk)
        mean = jnp.sum(conv, axis=1, keepdims=True) * (1.0 / width)
        cent = conv - mean
        var = jnp.sum(cent * cent, axis=1, keepdims=True) * (1.0 / width)
        rstd = lax.rsqrt(var + 1e-05)
        norm = cent * rstd
        pre = norm * par[5:6, :] + par[6:7, :]
        sig = 0.5 * jnp.tanh(0.5 * pre) + 0.5
        ids = base + lax.broadcasted_iota(jnp.int32, (chunk, 1), 0)
        out = jnp.where(ids < length, pre * sig, 0.0)
        swished[pl.ds(local, chunk), :] = out.astype(BF16)
        normed[pl.ds(local, chunk), :] = norm
        rstds[pl.ds(local, chunk), :] = jnp.broadcast_to(rstd, (chunk, 128))
        return 0

    lax.fori_loop(0, rows // chunk, one, 0, unroll=unroll)


def forward(lens, par, glu, rows=128, chunk=16, unroll=8):
    frames, width = glu.shape
    block = lambda w: pl.BlockSpec((rows, w), lambda i, *_: (i, 0))
    return pl.pallas_call(
        functools.partial(forward_kernel, rows=rows, frames=frames, chunk=chunk, unroll=unroll),
        out_shape=(sds((frames, width), BF16), sds((frames, width), F32), sds((frames, 128), F32)),
        grid_spec=pltpu.PrefetchScalarGridSpec(
            num_scalar_prefetch=1,
            grid=(frames // rows,),
            in_specs=[whole((8, width)), whole((frames, width))],
            out_specs=(block(width), block(width), block(128)),
            scratch_shapes=[pltpu.VMEM((frames + 2 * PAD, width), F32)],
        ),
        compiler_params=compiler(),
        name="forward",
        **params(0.1),
    )(lens, par, glu)


def outer_kernel(core, sw, cot, h1, h2, h3, keep, send):
    res = lax.dot_general(
        sw[...], cot[...], (((0,), (0,)), ((), ())), preferred_element_type=F32
    )
    first = core[0] == 0
    for j in range(4):
        a = res[j * 96 : j * 96 + 48]
        b = res[j * 96 + 48 : j * 96 + 96]
        keep[j] = jnp.where(first, a, b)
        send[j] = jnp.where(first, b, a).astype(BF16)


def outer(core, sw, cot, held):
    frames, width = sw.shape
    return pl.pallas_call(
        outer_kernel,
        out_shape=(sds((16, 48, width), F32), sds((16, 48, width), BF16)),
        grid_spec=pltpu.PrefetchScalarGridSpec(
            num_scalar_prefetch=1,
            grid=(4,),
            in_specs=[
                pl.BlockSpec((frames, 384), lambda i, *_: (0, i)),
                whole((frames, width)),
                HBM,
                HBM,
                HBM,
            ],
            out_specs=(
                pl.BlockSpec((4, 48, width), lambda i, *_: (i, 0, 0)),
                pl.BlockSpec((4, 48, width), lambda i, *_: (i, 0, 0)),
            ),
        ),
        compiler_params=compiler(),
        name="outer",
        **params(0.1),
    )(core, sw, cot, *held)


def stage1_kernel(pos, keep, recv, a0, a1, a2, a3):
    j = pl.program_id(0)
    for n, out in enumerate((a0, a1, a2, a3)):

        @pl.when(j == n)
        def _(out=out):
            out[...] = (keep[0] + recv[0].astype(F32)).astype(out.dtype)


def stage1(pos, keep, recv):
    width = keep.shape[-1]
    keep = keep.reshape(4, 4, 48, width)
    recv = recv.reshape(4, 4, 48, width)
    src = pl.BlockSpec((1, 4, 48, width), lambda j, pos: (pos[0] ^ j, 0, 0, 0))
    return pl.pallas_call(
        stage1_kernel,
        out_shape=tuple(sds((4, 48, width), t) for t in (F32, BF16, BF16, BF16)),
        grid_spec=pltpu.PrefetchScalarGridSpec(
            num_scalar_prefetch=1,
            grid=(4,),
            in_specs=[src, src],
            out_specs=(whole((4, 48, width)),) * 4,
        ),
        compiler_params=compiler(),
        name="stage1",
        **params(0.1),
    )(pos, keep, recv)


def stage2_kernel(pos, a0, a1, a2, a3, held, o0, o1, o2, o3):
    j = pl.program_id(0)
    for n, out in enumerate((o0, o1, o2, o3)):

        @pl.when(j == n)
        def _(out=out):
            total = (a0[0] + a1[0].astype(F32)) + (a2[0].astype(F32) + a3[0].astype(F32))
            out[...] = total.astype(out.dtype)


def stage2(pos, a, held):
    width = a[0].shape[-1]
    src = pl.BlockSpec((1, 48, width), lambda j, pos: (pos[2] ^ j, 0, 0))
    return pl.pallas_call(
        stage2_kernel,
        out_shape=tuple(sds((48, width), t) for t in (F32, BF16, BF16, BF16)),
        grid_spec=pltpu.PrefetchScalarGridSpec(
            num_scalar_prefetch=1,
            grid=(4,),
            in_specs=[src] * 4 + [HBM],
            out_specs=(whole((48, width)),) * 4,
        ),
        compiler_params=compiler(),
        name="stage2",
        **params(3),
    )(pos, *a, held)


def stage3_kernel(pos, v0, v1, v2, v3, held, o0, o1, o2, o3, total):
    total[...] = (v0[...] + v1[...].astype(F32)) + (v2[...].astype(F32) + v3[...].astype(F32))
    for n, out in enumerate((o0, o1, o2, o3)):
        at = pl.multiple_of((pos[1] ^ n) * 384, 128)
        out[...] = total[:, pl.ds(at, 384)]


def stage3(pos, v, held):
    shape = v[0].shape
    part = (shape[0], 384)
    return pl.pallas_call(
        stage3_kernel,
        out_shape=(sds(part, F32),) * 4,
        grid_spec=pltpu.PrefetchScalarGridSpec(
            num_scalar_prefetch=1,
            grid=(1,),
            in_specs=[whole(shape)] * 4 + [HBM],
            out_specs=(whole(part),) * 4,
            scratch_shapes=[pltpu.VMEM(shape, F32)],
        ),
        compiler_params=compiler(),
        name="stage3",
        **params(2),
    )(pos, *v, held)


def join_kernel(pos, v0, v1, v2, v3, out):
    for n, v in enumerate((v0, v1, v2, v3)):
        at = pl.multiple_of((pos[1] ^ n) * 384, 128)
        out[:, pl.ds(at, 384)] = v[...]


def join(pos, parts):
    rows = parts[0].shape[0]
    return pl.pallas_call(
        join_kernel,
        out_shape=sds((rows, 1536), F32),
        grid_spec=pltpu.PrefetchScalarGridSpec(
            num_scalar_prefetch=1,
            grid=(1,),
            in_specs=[whole((rows, 384))] * 4,
            out_specs=whole((rows, 1536)),
        ),
        compiler_params=compiler(),
        name="join",
        **params(2),
    )(pos, *parts)


def gather_kernel(w0, w1, w2, w3, held, out):
    rows = w0.shape[0]
    for n, w in enumerate((w0, w1, w2, w3)):
        out[n * rows : n * rows + rows, :] = w[...]


def gather(w, held):
    rows, width = w[0].shape
    return pl.pallas_call(
        gather_kernel,
        out_shape=sds((4 * rows, width), BF16),
        grid=(1,),
        in_specs=[whole((rows, width))] * 4 + [HBM],
        out_specs=whole((4 * rows, width)),
        compiler_params=compiler(),
        name="gather",
        **params(0.1),
    )(*w, held)


def fetch_weight(pos, pieces, buf, sem):
    y, z, core = pos[0], pos[2], pos[3]
    copies = []
    for n, piece in enumerate(pieces):
        for j in range(16):
            index = ((y ^ (j // 4)) * 4 + (z ^ (j % 4))) * 2 + (core ^ n)
            at = pl.multiple_of(index * 48, 48)
            copies.append(
                pltpu.make_async_copy(
                    piece.at[pl.ds(j * 48, 48), :], buf.at[pl.ds(at, 48), :], sem.at[n * 16 + j]
                )
            )
    for c in copies:
        c.start()
    for c in copies:
        c.wait()


def project_kernel(pos, *refs):
    pieces, (sw, res, _, _, out, buf, sem) = refs[:2], refs[2:]

    @pl.when(pl.program_id(0) == 0)
    def _():
        fetch_weight(pos, pieces, buf, sem)

    prod = jnp.dot(sw[...], buf[...], preferred_element_type=F32)
    out[...] = (res[...].astype(F32) + prod).astype(BF16)


def project(pos, pieces, sw, res, held, rows=256):
    frames, width = sw.shape
    block = pl.BlockSpec((rows, width), lambda i, *_: (i, 0))
    return pl.pallas_call(
        project_kernel,
        out_shape=sds((frames, width), BF16),
        grid_spec=pltpu.PrefetchScalarGridSpec(
            num_scalar_prefetch=1,
            grid=(frames // rows,),
            in_specs=[HBM] * 2 + [block, block, HBM, HBM],
            out_specs=block,
            scratch_shapes=[pltpu.VMEM((width, width), BF16), pltpu.SemaphoreType.DMA((32,))],
        ),
        compiler_params=compiler(),
        name="project",
        **params(11),
    )(pos, *pieces, sw, res, *held)


def backward_kernel(pos, *refs, rows, chunk, unroll):
    pieces = refs[:2]
    par, cot, nrm, rst, _, gconv, sums, buf, sem, grad = refs[2:]
    step = pl.program_id(0)
    width = cot.shape[1]
    length = pos[4]

    @pl.when(step == 0)
    def _():
        fetch_weight(pos, pieces, buf, sem)
        sums[...] = jnp.zeros_like(sums)

    grad[...] = lax.dot_general(
        cot[...], buf[...], (((1,), (1,)), ((), ())), preferred_element_type=F32
    )

    def one(i, _):
        at = pl.multiple_of(i * chunk, chunk)
        gain = par[5:6, :]
        norm = nrm[pl.ds(at, chunk), :]
        pre = norm * gain + par[6:7, :]
        sig = 0.5 * jnp.tanh(0.5 * pre) + 0.5
        ids = step * rows + at + lax.broadcasted_iota(jnp.int32, (chunk, 1), 0)
        gs = jnp.where(ids < length, grad[pl.ds(at, chunk), :], 0.0)
        gpre = gs * (sig * (1.0 + pre * (1.0 - sig)))
        gn = gpre * norm
        for h in range(chunk // 8):
            sums[0] += gn[h * 8 : h * 8 + 8]
            sums[1] += gpre[h * 8 : h * 8 + 8]
        gnorm = gpre * gain
        m1 = jnp.sum(gnorm, axis=1, keepdims=True) * (1.0 / width)
        m2 = jnp.sum(gnorm * norm, axis=1, keepdims=True) * (1.0 / width)
        gconv[pl.ds(at, chunk), :] = rst[pl.ds(at, chunk), 0:1] * (gnorm - m1 - norm * m2)
        return 0

    lax.fori_loop(0, rows // chunk, one, 0, unroll=unroll)


def backward(pos, pieces, par, cot, nrm, rst, held, rows=256, chunk=16, unroll=4):
    frames, width = cot.shape
    block = lambda w: pl.BlockSpec((rows, w), lambda i, *_: (i, 0))
    return pl.pallas_call(
        functools.partial(backward_kernel, rows=rows, chunk=chunk, unroll=unroll),
        out_shape=(sds((frames, width), F32), sds((2, 8, width), F32)),
        grid_spec=pltpu.PrefetchScalarGridSpec(
            num_scalar_prefetch=1,
            grid=(frames // rows,),
            in_specs=[HBM] * 2
            + [whole((8, width)), block(width), block(width), block(128), HBM],
            out_specs=(block(width), whole((2, 8, width))),
            scratch_shapes=[
                pltpu.VMEM((width, width), BF16),
                pltpu.SemaphoreType.DMA((32,)),
                pltpu.VMEM((rows, width), F32),
            ],
        ),
        compiler_params=compiler(),
        name="backward",
        **params(21),
    )(pos, *pieces, par, cot, nrm, rst, held)


def taps_kernel(pos, par, glu, gconv, norm_sums, out, small, pad, sums, *, rows, frames, chunk, unroll, strip):
    step = pl.program_id(0)
    width = glu.shape[1]
    length = pos[4]

    @pl.when(step == 0)
    def _():
        sums[...] = jnp.zeros_like(sums)
        pad[pl.ds(0, PAD), :] = jnp.zeros((PAD, width), F32)
        pad[pl.ds(PAD + frames, PAD), :] = jnp.zeros((PAD, width), F32)

    @pl.when(step < frames // rows)
    def _():
        pad[pl.ds(pl.multiple_of(PAD + step * rows, 8), rows), :] = gconv[...]

    @pl.when(step > 0)
    def _():
        start = (step - 1) * rows
        for c in range(0, width, strip):
            cols = slice(c, c + strip)

            def one(i, acc, cols=cols):
                at = pl.multiple_of(i * chunk, chunk)
                base = pl.multiple_of(start + at, 8)
                live = base + lax.broadcasted_iota(jnp.int32, (chunk, 1), 0) < length
                mk = jnp.where(live, glu[pl.ds(at, chunk), cols].astype(F32), 0.0)
                near = pad[pl.ds(base, chunk + 2 * PAD), cols]
                grad, new = None, []
                for k in range(TAPS):
                    g = shifted(near, 2 - k, chunk)
                    term = par[k : k + 1, cols] * g
                    grad = term if grad is None else grad + term
                    p = mk * g
                    new.append(acc[k] + sum(p[h : h + 8] for h in range(0, chunk, 8)))
                out[pl.ds(at, chunk), cols] = jnp.where(live, grad, 0.0).astype(BF16)
                return tuple(new)

            zero = jnp.zeros((8, strip), F32)
            acc = lax.fori_loop(0, rows // chunk, one, (zero,) * TAPS, unroll=unroll)
            for k in range(TAPS):
                sums[k, :, cols] += acc[k]

    @pl.when(step == frames // rows)
    def _():
        for k in range(TAPS):
            small[k : k + 1, :] = jnp.sum(sums[k], axis=0, keepdims=True)
        for k in range(2):
            small[TAPS + k : TAPS + k + 1, :] = jnp.sum(norm_sums[k], axis=0, keepdims=True)
        small[TAPS + 2 :, :] = jnp.zeros((1, width), F32)


def taps(pos, par, glu, gconv, norm_sums, rows=128, chunk=32, unroll=2, strip=256):
    frames, width = glu.shape
    last = frames // rows - 1
    late = pl.BlockSpec((rows, width), lambda i, *_: (jnp.maximum(i - 1, 0), 0))
    return pl.pallas_call(
        functools.partial(taps_kernel, rows=rows, frames=frames, chunk=chunk, unroll=unroll, strip=strip),
        out_shape=(sds((frames, width), BF16), sds((8, width), F32)),
        grid_spec=pltpu.PrefetchScalarGridSpec(
            num_scalar_prefetch=1,
            grid=(frames // rows + 1,),
            in_specs=[
                whole((8, width)),
                late,
                pl.BlockSpec((rows, width), lambda i, *_: (jnp.minimum(i, last), 0)),
                whole((2, 8, width)),
            ],
            out_specs=(late, whole((8, width))),
            scratch_shapes=[pltpu.VMEM((frames + 2 * PAD, width), F32), pltpu.VMEM((TAPS, 8, width), F32)],
        ),
        compiler_params=compiler(),
        name="taps",
        **params(10),
    )(pos, par, glu, gconv, norm_sums)


def local(glu_out, residual_in, cotangent, lengths, conv_kernel, norm_gain, norm_bias, proj_weight):
    _, frames, width = glu_out.shape
    glu, res, cot = glu_out[0], residual_in[0], cotangent[0]
    f, d = lax.axis_index("fsdp"), lax.axis_index("dp")
    core, z, y = f % 2, (f // 2) % 4, f // 8
    x = d % 4
    pos = jnp.stack([y, x, z, core, lengths[0]]).astype(jnp.int32)

    own = jnp.concatenate([conv_kernel, norm_gain[None], norm_bias[None]], axis=0)
    own = jnp.pad(own, ((0, 1), (0, 0)))
    par = lax.dynamic_update_slice(jnp.zeros((8, width), BF16), own, (0, f * 48))
    par = par + fsdp_move(par, core=1)
    par = (par + fsdp_move(par, y=1)) + (fsdp_move(par, y=2) + fsdp_move(par, y=3))
    par = par + fsdp_move(par, z=1)
    par = par + fsdp_move(par, z=3)
    par = par.astype(F32)

    block = gather([proj_weight] + [fsdp_move(proj_weight, z=k) for k in (1, 2, 3)], own)
    near = [block] + [fsdp_move(block, y=k) for k in (1, 2, 3)]

    swished, normed, rstd = forward(lengths, par, glu)
    keep, send = outer(core[None].astype(jnp.int32), swished, cot, near[1:])
    recv = fsdp_move(send, core=1)
    a = stage1(pos, keep, recv)
    mine = gather(near, a[0])
    pieces = [mine, fsdp_move(mine, core=1)]
    gconv, sums = backward(pos, pieces, par, cot, normed, rstd, a[0])
    glu_grad, small = taps(pos, par, glu, gconv, sums)
    v = stage2(pos, [a[0]] + [fsdp_move(a[k], y=k) for k in (1, 2, 3)], glu_grad)
    small = small + fsdp_move(small, core=1)
    small = (small + fsdp_move(small, y=1)) + (fsdp_move(small, y=2) + fsdp_move(small, y=3))
    block_out = project(pos, pieces, swished, res, (v[0], small))
    v = stage3(pos, [v[0]] + [fsdp_move(v[k], z=k) for k in (1, 2, 3)], block_out)
    total = (v[0] + dp_move(v[1], x=1)) + (dp_move(v[2], x=2) + dp_move(v[3], x=3))
    total = total + dp_move(total, low=1)
    proj_grad = join(pos, [total] + [dp_move(total, x=k) for k in (1, 2, 3)])

    small = small + fsdp_move(small, z=1)
    small = small + fsdp_move(small, z=3)
    small = lax.dynamic_slice(small, (0, f * 48), (8, 48))
    small = (small + dp_move(small, x=1)) + (dp_move(small, x=2) + dp_move(small, x=3))
    small = small + dp_move(small, low=1)
    return (block_out[None], glu_grad[None], proj_grad, small[:TAPS], small[TAPS : TAPS + 2])


def solution(mesh):
    rows = P(("dp", "fsdp"), None, None)
    return jax.shard_map(
        local,
        mesh=mesh,
        in_specs=(rows, rows, rows, P(("dp", "fsdp")), P(None, "fsdp"), P("fsdp"), P("fsdp"), P("fsdp", None)),
        out_specs=(rows, rows, P("fsdp", None), P(None, "fsdp"), P(None, "fsdp")),
        check_vma=False,
    )
```

```python
import functools

import jax
import jax.numpy as jnp
from jax import lax
from jax.experimental import pallas as pl
from jax.experimental.pallas import tpu as pltpu
from jax.sharding import PartitionSpec as P

TAPS = 5
NX, NY, NZ = 4, 4, 4
F32, BF16 = jnp.float32, jnp.bfloat16
PAD = 8
HBM = pl.BlockSpec(memory_space=pl.ANY)
VMEM_LIMIT = 60 * 1024 * 1024


def fsdp_move(value, y=0, z=0, core=0):
    perm = [(i, i ^ (y * 8 + z * 2 + core)) for i in range(32)]
    return lax.ppermute(value, "fsdp", perm)


def dp_move(value, x=0, low=0):
    perm = [(i, i ^ (low * 4 + x)) for i in range(8)]
    return lax.ppermute(value, "dp", perm)


def params(micros):
    return dict(
        cost_estimate=pl.CostEstimate(flops=0, bytes_accessed=int(micros * 3.6e6), transcendentals=0),
    )


def compiler():
    return pltpu.CompilerParams(vmem_limit_bytes=VMEM_LIMIT)


def shifted(near, by, count):
    if by != 0:
        near = pltpu.roll(near, (-by) % near.shape[0], 0)
    return near[PAD : PAD + count]


def sds(shape, dtype):
    return jax.ShapeDtypeStruct(shape, dtype)


def whole(shape):
    return pl.BlockSpec(shape, lambda *_: (0,) * len(shape))


def forward_kernel(lens, par, glu, swished, normed, rstds, masked, *, rows, frames, chunk, unroll):
    step = pl.program_id(0)
    length = lens[0]
    width = glu.shape[1]

    @pl.when(step == 0)
    def _():
        masked[pl.ds(0, PAD), :] = jnp.zeros((PAD, width), F32)
        masked[pl.ds(PAD + frames, PAD), :] = jnp.zeros((PAD, width), F32)

        def fill(i, _):
            at = pl.multiple_of(i * 16, 16)
            ids = at + lax.broadcasted_iota(jnp.int32, (16, 1), 0)
            v = glu[pl.ds(at, 16), :].astype(F32)
            masked[pl.ds(pl.multiple_of(at + PAD, 8), 16), :] = jnp.where(ids < length, v, 0.0)
            return 0

        lax.fori_loop(0, frames // 16, fill, 0, unroll=4)

    def one(i, _):
        local = pl.multiple_of(i * chunk, chunk)
        base = step * rows + local
        near = masked[pl.ds(pl.multiple_of(base, 8), chunk + 2 * PAD), :]
        conv = par[0:1, :] * shifted(near, -2, chunk)
        for k in range(1, TAPS):
            conv = conv + par[k : k + 1, :] * shifted(near, k - 2, chunk)
        mean = jnp.sum(conv, axis=1, keepdims=True) * (1.0 / width)
        cent = conv - mean
        var = jnp.sum(cent * cent, axis=1, keepdims=True) * (1.0 / width)
        rstd = lax.rsqrt(var + 1e-05)
        norm = cent * rstd
        pre = norm * par[5:6, :] + par[6:7, :]
        sig = 0.5 * jnp.tanh(0.5 * pre) + 0.5
        ids = base + lax.broadcasted_iota(jnp.int32, (chunk, 1), 0)
        out = jnp.where(ids < length, pre * sig, 0.0)
        swished[pl.ds(local, chunk), :] = out.astype(BF16)
        normed[pl.ds(local, chunk), :] = norm
        rstds[pl.ds(local, chunk), :] = jnp.broadcast_to(rstd, (chunk, 128))
        return 0

    lax.fori_loop(0, rows // chunk, one, 0, unroll=unroll)


def forward(lens, par, glu, rows=128, chunk=16, unroll=8):
    frames, width = glu.shape
    block = lambda w: pl.BlockSpec((rows, w), lambda i, *_: (i, 0))
    return pl.pallas_call(
        functools.partial(forward_kernel, rows=rows, frames=frames, chunk=chunk, unroll=unroll),
        out_shape=(sds((frames, width), BF16), sds((frames, width), F32), sds((frames, 128), F32)),
        grid_spec=pltpu.PrefetchScalarGridSpec(
            num_scalar_prefetch=1,
            grid=(frames // rows,),
            in_specs=[whole((8, width)), whole((frames, width))],
            out_specs=(block(width), block(width), block(128)),
            scratch_shapes=[pltpu.VMEM((frames + 2 * PAD, width), F32)],
        ),
        compiler_params=compiler(),
        name="forward",
        **params(0.1),
    )(lens, par, glu)


def outer_kernel(core, sw, cot, h1, h2, h3, keep, send):
    res = lax.dot_general(
        sw[...], cot[...], (((0,), (0,)), ((), ())), preferred_element_type=F32
    )
    first = core[0] == 0
    for j in range(4):
        a = res[j * 96 : j * 96 + 48]
        b = res[j * 96 + 48 : j * 96 + 96]
        keep[j] = jnp.where(first, a, b)
        send[j] = jnp.where(first, b, a).astype(BF16)


def outer(core, sw, cot, held):
    frames, width = sw.shape
    return pl.pallas_call(
        outer_kernel,
        out_shape=(sds((16, 48, width), F32), sds((16, 48, width), BF16)),
        grid_spec=pltpu.PrefetchScalarGridSpec(
            num_scalar_prefetch=1,
            grid=(4,),
            in_specs=[
                pl.BlockSpec((frames, 384), lambda i, *_: (0, i)),
                whole((frames, width)),
                HBM,
                HBM,
                HBM,
            ],
            out_specs=(
                pl.BlockSpec((4, 48, width), lambda i, *_: (i, 0, 0)),
                pl.BlockSpec((4, 48, width), lambda i, *_: (i, 0, 0)),
            ),
        ),
        compiler_params=compiler(),
        name="outer",
        **params(0.1),
    )(core, sw, cot, *held)


def stage1_kernel(pos, keep, recv, a0, a1, a2, a3):
    j = pl.program_id(0)
    for n, out in enumerate((a0, a1, a2, a3)):

        @pl.when(j == n)
        def _(out=out):
            out[...] = (keep[0] + recv[0].astype(F32)).astype(out.dtype)


def stage1(pos, keep, recv):
    width = keep.shape[-1]
    keep = keep.reshape(4, 4, 48, width)
    recv = recv.reshape(4, 4, 48, width)
    src = pl.BlockSpec((1, 4, 48, width), lambda j, pos: (pos[0] ^ j, 0, 0, 0))
    return pl.pallas_call(
        stage1_kernel,
        out_shape=tuple(sds((4, 48, width), t) for t in (F32, BF16, BF16, BF16)),
        grid_spec=pltpu.PrefetchScalarGridSpec(
            num_scalar_prefetch=1,
            grid=(4,),
            in_specs=[src, src],
            out_specs=(whole((4, 48, width)),) * 4,
        ),
        compiler_params=compiler(),
        name="stage1",
        **params(0.1),
    )(pos, keep, recv)


def stage2_kernel(pos, a0, a1, a2, a3, small, o0, o1, o2, o3, same):
    j = pl.program_id(0)
    same[...] = small[...]
    for n, out in enumerate((o0, o1, o2, o3)):

        @pl.when(j == n)
        def _(out=out):
            total = (a0[0] + a1[0].astype(F32)) + (a2[0].astype(F32) + a3[0].astype(F32))
            out[...] = total.astype(out.dtype)


def stage2(pos, a, small):
    width = a[0].shape[-1]
    src = pl.BlockSpec((1, 48, width), lambda j, pos: (pos[2] ^ j, 0, 0))
    return pl.pallas_call(
        stage2_kernel,
        out_shape=tuple(sds((48, width), t) for t in (F32, BF16, BF16, BF16)) + (sds(small.shape, F32),),
        grid_spec=pltpu.PrefetchScalarGridSpec(
            num_scalar_prefetch=1,
            grid=(4,),
            in_specs=[src] * 4 + [whole(small.shape)],
            out_specs=(whole((48, width)),) * 4 + (whole(small.shape),),
        ),
        compiler_params=compiler(),
        name="stage2",
        **params(3),
    )(pos, *a, small)


def stage3_kernel(pos, v0, v1, v2, v3, small, o0, o1, o2, o3, total):
    total[...] = (v0[...] + v1[...].astype(F32)) + (v2[...].astype(F32) + v3[...].astype(F32))
    for n, out in enumerate((o0, o1, o2, o3)):
        at = pl.multiple_of((pos[1] ^ n) * 384, 128)
        out[0:48, :] = total[:, pl.ds(at, 384)]
        out[48:56, :] = small[...]


def stage3(pos, v, small):
    shape = v[0].shape
    part = (shape[0] + 8, 384)
    return pl.pallas_call(
        stage3_kernel,
        out_shape=(sds(part, F32),) * 4,
        grid_spec=pltpu.PrefetchScalarGridSpec(
            num_scalar_prefetch=1,
            grid=(1,),
            in_specs=[whole(shape)] * 4 + [whole(small.shape)],
            out_specs=(whole(part),) * 4,
            scratch_shapes=[pltpu.VMEM(shape, F32)],
        ),
        compiler_params=compiler(),
        name="stage3",
        **params(2),
    )(pos, *v, small)


def join_kernel(pos, v0, v1, v2, v3, out):
    for n, v in enumerate((v0, v1, v2, v3)):
        at = pl.multiple_of((pos[1] ^ n) * 384, 128)
        out[:, pl.ds(at, 384)] = v[0:48, :]


def join(pos, parts):
    rows = parts[0].shape[0] - 8
    return pl.pallas_call(
        join_kernel,
        out_shape=sds((rows, 1536), F32),
        grid_spec=pltpu.PrefetchScalarGridSpec(
            num_scalar_prefetch=1,
            grid=(1,),
            in_specs=[whole((rows + 8, 384))] * 4,
            out_specs=whole((rows, 1536)),
        ),
        compiler_params=compiler(),
        name="join",
        **params(2),
    )(pos, *parts)


def gather_kernel(w0, w1, w2, w3, held, out):
    rows = w0.shape[0]
    for n, w in enumerate((w0, w1, w2, w3)):
        out[n * rows : n * rows + rows, :] = w[...]


def gather(w, held):
    rows, width = w[0].shape
    return pl.pallas_call(
        gather_kernel,
        out_shape=sds((4 * rows, width), BF16),
        grid=(1,),
        in_specs=[whole((rows, width))] * 4 + [HBM],
        out_specs=whole((4 * rows, width)),
        compiler_params=compiler(),
        name="gather",
        **params(0.1),
    )(*w, held)


def fetch_weight(pos, pieces, buf, sem):
    y, z, core = pos[0], pos[2], pos[3]
    copies = []
    for n, piece in enumerate(pieces):
        dc, dy = n // 4, n % 4
        for dz in range(4):
            index = ((y ^ dy) * 4 + (z ^ dz)) * 2 + (core ^ dc)
            at = pl.multiple_of(index * 48, 48)
            copies.append(
                pltpu.make_async_copy(
                    piece.at[pl.ds(dz * 48, 48), :], buf.at[pl.ds(at, 48), :], sem.at[n * 4 + dz]
                )
            )
    for c in copies:
        c.start()
    for c in copies:
        c.wait()


def project_kernel(pos, *refs):
    pieces, (sw, res, _, _, out, buf, sem) = refs[:8], refs[8:]

    @pl.when(pl.program_id(0) == 0)
    def _():
        fetch_weight(pos, pieces, buf, sem)

    prod = jnp.dot(sw[...], buf[...], preferred_element_type=F32)
    out[...] = (res[...].astype(F32) + prod).astype(BF16)


def project(pos, pieces, sw, res, held, rows=256):
    frames, width = sw.shape
    block = pl.BlockSpec((rows, width), lambda i, *_: (i, 0))
    return pl.pallas_call(
        project_kernel,
        out_shape=sds((frames, width), BF16),
        grid_spec=pltpu.PrefetchScalarGridSpec(
            num_scalar_prefetch=1,
            grid=(frames // rows,),
            in_specs=[HBM] * 8 + [block, block, HBM, HBM],
            out_specs=block,
            scratch_shapes=[pltpu.VMEM((width, width), BF16), pltpu.SemaphoreType.DMA((32,))],
        ),
        compiler_params=compiler(),
        name="project",
        **params(11),
    )(pos, *pieces, sw, res, *held)


def backward_kernel(pos, *refs, rows, chunk, unroll):
    pieces = refs[:8]
    par, cot, nrm, rst, _, gconv, sums, buf, sem, grad = refs[8:]
    step = pl.program_id(0)
    width = cot.shape[1]
    length = pos[4]

    @pl.when(step == 0)
    def _():
        fetch_weight(pos, pieces, buf, sem)
        sums[...] = jnp.zeros_like(sums)

    grad[...] = lax.dot_general(
        cot[...], buf[...], (((1,), (1,)), ((), ())), preferred_element_type=F32
    )

    def one(i, _):
        at = pl.multiple_of(i * chunk, chunk)
        gain = par[5:6, :]
        norm = nrm[pl.ds(at, chunk), :]
        pre = norm * gain + par[6:7, :]
        sig = 0.5 * jnp.tanh(0.5 * pre) + 0.5
        ids = step * rows + at + lax.broadcasted_iota(jnp.int32, (chunk, 1), 0)
        gs = jnp.where(ids < length, grad[pl.ds(at, chunk), :], 0.0)
        gpre = gs * (sig * (1.0 + pre * (1.0 - sig)))
        gn = gpre * norm
        for h in range(chunk // 8):
            sums[0] += gn[h * 8 : h * 8 + 8]
            sums[1] += gpre[h * 8 : h * 8 + 8]
        gnorm = gpre * gain
        m1 = jnp.sum(gnorm, axis=1, keepdims=True) * (1.0 / width)
        m2 = jnp.sum(gnorm * norm, axis=1, keepdims=True) * (1.0 / width)
        gconv[pl.ds(at, chunk), :] = rst[pl.ds(at, chunk), 0:1] * (gnorm - m1 - norm * m2)
        return 0

    lax.fori_loop(0, rows // chunk, one, 0, unroll=unroll)


def backward(pos, pieces, par, cot, nrm, rst, held, rows=256, chunk=16, unroll=4):
    frames, width = cot.shape
    block = lambda w: pl.BlockSpec((rows, w), lambda i, *_: (i, 0))
    return pl.pallas_call(
        functools.partial(backward_kernel, rows=rows, chunk=chunk, unroll=unroll),
        out_shape=(sds((frames, width), F32), sds((2, 8, width), F32)),
        grid_spec=pltpu.PrefetchScalarGridSpec(
            num_scalar_prefetch=1,
            grid=(frames // rows,),
            in_specs=[HBM] * 8
            + [whole((8, width)), block(width), block(width), block(128), HBM],
            out_specs=(block(width), whole((2, 8, width))),
            scratch_shapes=[
                pltpu.VMEM((width, width), BF16),
                pltpu.SemaphoreType.DMA((32,)),
                pltpu.VMEM((rows, width), F32),
            ],
        ),
        compiler_params=compiler(),
        name="backward",
        **params(0.1),
    )(pos, *pieces, par, cot, nrm, rst, held)


def taps_kernel(pos, par, glu, gconv, norm_sums, out, small, pad, sums, *, rows, frames, chunk, unroll, strip):
    step = pl.program_id(0)
    width = glu.shape[1]
    length = pos[4]

    @pl.when(step == 0)
    def _():
        sums[...] = jnp.zeros_like(sums)
        pad[pl.ds(0, PAD), :] = jnp.zeros((PAD, width), F32)
        pad[pl.ds(PAD + frames, PAD), :] = jnp.zeros((PAD, width), F32)

    @pl.when(step < frames // rows)
    def _():
        pad[pl.ds(pl.multiple_of(PAD + step * rows, 8), rows), :] = gconv[...]

    @pl.when(step > 0)
    def _():
        start = (step - 1) * rows
        for c in range(0, width, strip):
            cols = slice(c, c + strip)

            def one(i, acc, cols=cols):
                at = pl.multiple_of(i * chunk, chunk)
                base = pl.multiple_of(start + at, 8)
                live = base + lax.broadcasted_iota(jnp.int32, (chunk, 1), 0) < length
                mk = jnp.where(live, glu[pl.ds(at, chunk), cols].astype(F32), 0.0)
                near = pad[pl.ds(base, chunk + 2 * PAD), cols]
                grad, new = None, []
                for k in range(TAPS):
                    g = shifted(near, 2 - k, chunk)
                    term = par[k : k + 1, cols] * g
                    grad = term if grad is None else grad + term
                    p = mk * g
                    new.append(acc[k] + sum(p[h : h + 8] for h in range(0, chunk, 8)))
                out[pl.ds(at, chunk), cols] = jnp.where(live, grad, 0.0).astype(BF16)
                return tuple(new)

            zero = jnp.zeros((8, strip), F32)
            acc = lax.fori_loop(0, rows // chunk, one, (zero,) * TAPS, unroll=unroll)
            for k in range(TAPS):
                sums[k, :, cols] += acc[k]

    @pl.when(step == frames // rows)
    def _():
        for k in range(TAPS):
            small[k : k + 1, :] = jnp.sum(sums[k], axis=0, keepdims=True)
        for k in range(2):
            small[TAPS + k : TAPS + k + 1, :] = jnp.sum(norm_sums[k], axis=0, keepdims=True)
        small[TAPS + 2 :, :] = jnp.zeros((1, width), F32)


def taps(pos, par, glu, gconv, norm_sums, rows=128, chunk=32, unroll=2, strip=256):
    frames, width = glu.shape
    last = frames // rows - 1
    late = pl.BlockSpec((rows, width), lambda i, *_: (jnp.maximum(i - 1, 0), 0))
    return pl.pallas_call(
        functools.partial(taps_kernel, rows=rows, frames=frames, chunk=chunk, unroll=unroll, strip=strip),
        out_shape=(sds((frames, width), BF16), sds((8, width), F32)),
        grid_spec=pltpu.PrefetchScalarGridSpec(
            num_scalar_prefetch=1,
            grid=(frames // rows + 1,),
            in_specs=[
                whole((8, width)),
                late,
                pl.BlockSpec((rows, width), lambda i, *_: (jnp.minimum(i, last), 0)),
                whole((2, 8, width)),
            ],
            out_specs=(late, whole((8, width))),
            scratch_shapes=[pltpu.VMEM((frames + 2 * PAD, width), F32), pltpu.VMEM((TAPS, 8, width), F32)],
        ),
        compiler_params=compiler(),
        name="taps",
        **params(10),
    )(pos, par, glu, gconv, norm_sums)


def finish_kernel(pos, *refs, rows, frames, chunk, strip):
    pieces = refs[:8]
    par, glu, gconv, norm_sums, sw, res, grad, out, small, buf, sem, pad, sums = refs[8:]
    step = pl.program_id(0)
    width = glu.shape[1]
    length = pos[4]
    last = frames // rows

    @pl.when(step == 0)
    def _():
        fetch_weight(pos, pieces, buf, sem)
        pad[pl.ds(0, PAD), :] = jnp.zeros((PAD, width), F32)
        pad[pl.ds(PAD + frames, PAD), :] = jnp.zeros((PAD, width), F32)

    @pl.when(step < 2)
    def _():
        sums[...] = jnp.zeros_like(sums)

    @pl.when(step < last)
    def _():
        pad[pl.ds(pl.multiple_of(PAD + step * rows, 8), rows), :] = gconv[...]

    start = jnp.maximum(step - 1, 0) * rows
    for c in range(0, width, strip):
        cols = slice(c, c + strip)
        prod = jnp.dot(sw[...], buf[:, cols], preferred_element_type=F32)
        out[:, cols] = (res[:, cols].astype(F32) + prod).astype(BF16)
        acc = [jnp.zeros((8, strip), F32)] * TAPS
        for at in range(0, rows, chunk):
            base = pl.multiple_of(start + at, 8)
            live = base + lax.broadcasted_iota(jnp.int32, (chunk, 1), 0) < length
            mk = jnp.where(live, glu[pl.ds(at, chunk), cols].astype(F32), 0.0)
            near = pad[pl.ds(base, chunk + 2 * PAD), cols]
            total = None
            for k in range(TAPS):
                g = shifted(near, 2 - k, chunk)
                term = par[k : k + 1, cols] * g
                total = term if total is None else total + term
                p = mk * g
                acc[k] = acc[k] + sum(p[h : h + 8] for h in range(0, chunk, 8))
            grad[pl.ds(at, chunk), cols] = jnp.where(live, total, 0.0).astype(BF16)
        for k in range(TAPS):
            sums[k, :, cols] += acc[k]

    @pl.when(step == last)
    def _():
        for k in range(TAPS):
            small[k : k + 1, :] = jnp.sum(sums[k], axis=0, keepdims=True)
        for k in range(2):
            small[TAPS + k : TAPS + k + 1, :] = jnp.sum(norm_sums[k], axis=0, keepdims=True)
        small[TAPS + 2 :, :] = jnp.zeros((1, width), F32)


def finish(pos, pieces, par, glu, gconv, norm_sums, sw, res, rows=256, chunk=32, strip=256):
    frames, width = glu.shape
    last = frames // rows - 1
    late = pl.BlockSpec((rows, width), lambda i, *_: (jnp.maximum(i - 1, 0), 0))
    soon = pl.BlockSpec((rows, width), lambda i, *_: (jnp.minimum(i, last), 0))
    return pl.pallas_call(
        functools.partial(finish_kernel, rows=rows, frames=frames, chunk=chunk, strip=strip),
        out_shape=(sds((frames, width), BF16), sds((frames, width), BF16), sds((8, width), F32)),
        grid_spec=pltpu.PrefetchScalarGridSpec(
            num_scalar_prefetch=1,
            grid=(frames // rows + 1,),
            in_specs=[HBM] * 8 + [whole((8, width)), late, soon, whole((2, 8, width)), soon, soon],
            out_specs=(late, soon, whole((8, width))),
            scratch_shapes=[
                pltpu.VMEM((width, width), BF16),
                pltpu.SemaphoreType.DMA((32,)),
                pltpu.VMEM((frames + 2 * PAD, width), F32),
                pltpu.VMEM((TAPS, 8, width), F32),
            ],
        ),
        compiler_params=compiler(),
        name="finish",
        **params(0.1),
    )(pos, *pieces, par, glu, gconv, norm_sums, sw, res)


def hold_kernel(a, b, h1, h2, h3, out):
    out[...] = a[...] + b[...]


def hold_add(a, b, held):
    return pl.pallas_call(
        hold_kernel,
        out_shape=sds(a.shape, a.dtype),
        grid=(1,),
        in_specs=[whole(a.shape)] * 2 + [HBM] * 3,
        out_specs=whole(a.shape),
        compiler_params=compiler(),
        name="hold_add",
        **params(1),
    )(a, b, *held)


def local(glu_out, residual_in, cotangent, lengths, conv_kernel, norm_gain, norm_bias, proj_weight):
    _, frames, width = glu_out.shape
    glu, res, cot = glu_out[0], residual_in[0], cotangent[0]
    f, d = lax.axis_index("fsdp"), lax.axis_index("dp")
    core, z, y = f % 2, (f // 2) % 4, f // 8
    x = d % 4
    pos = jnp.stack([y, x, z, core, lengths[0]]).astype(jnp.int32)

    own = jnp.concatenate([conv_kernel, norm_gain[None], norm_bias[None]], axis=0)
    own = jnp.pad(own, ((0, 1), (0, 0)))
    par = lax.dynamic_update_slice(jnp.zeros((8, width), BF16), own, (0, f * 48))
    par = par + fsdp_move(par, core=1)
    par = (par + fsdp_move(par, y=1)) + (fsdp_move(par, y=2) + fsdp_move(par, y=3))
    par = par + fsdp_move(par, z=1)
    par = par + fsdp_move(par, z=3)
    par = par.astype(F32)

    block = gather([proj_weight] + [fsdp_move(proj_weight, z=k) for k in (1, 2, 3)], own)
    near = [block] + [fsdp_move(block, y=k) for k in (1, 2, 3)]
    pieces = near + [fsdp_move(p, core=1) for p in near]

    swished, normed, rstd = forward(lengths, par, glu)
    keep, send = outer(core[None].astype(jnp.int32), swished, cot, near[1:])
    recv = fsdp_move(send, core=1)
    a = stage1(pos, keep, recv)
    gconv, sums = backward(pos, pieces, par, cot, normed, rstd, a[0])
    glu_grad, block_out, small = finish(pos, pieces, par, glu, gconv, sums, swished, res)
    *v, small = stage2(pos, [a[0]] + [fsdp_move(a[k], y=k) for k in (1, 2, 3)], small)
    small = small + fsdp_move(small, core=1)
    small = (small + fsdp_move(small, y=1)) + (fsdp_move(small, y=2) + fsdp_move(small, y=3))
    v = [v[0]] + [fsdp_move(v[k], z=k) for k in (1, 2, 3)]
    small = hold_add(small, fsdp_move(small, z=1), v[1:])
    small = small + fsdp_move(small, z=3)
    small = jnp.pad(lax.dynamic_slice(small, (0, f * 48), (8, 48)), ((0, 0), (0, 336)))
    v = stage3(pos, v, small)
    total = (v[0] + dp_move(v[1], x=1)) + (dp_move(v[2], x=2) + dp_move(v[3], x=3))
    total = total + dp_move(total, low=1)
    proj_grad = join(pos, [total] + [dp_move(total, x=k) for k in (1, 2, 3)])
    small = total[48:, :48]
    return (block_out[None], glu_grad[None], proj_grad, small[:TAPS], small[TAPS : TAPS + 2])


def solution(mesh):
    rows = P(("dp", "fsdp"), None, None)
    return jax.shard_map(
        local,
        mesh=mesh,
        in_specs=(rows, rows, rows, P(("dp", "fsdp")), P(None, "fsdp"), P("fsdp"), P("fsdp"), P("fsdp", None)),
        out_specs=(rows, rows, P("fsdp", None), P(None, "fsdp"), P(None, "fsdp")),
        check_vma=False,
    )
```

```python
import functools

import jax
import jax.numpy as jnp
from jax import lax
from jax.experimental import pallas as pl
from jax.experimental.pallas import tpu as pltpu
from jax.sharding import PartitionSpec as P

TAPS = 5
NX, NY, NZ = 4, 4, 4
F32, BF16 = jnp.float32, jnp.bfloat16
PAD = 8
HBM = pl.BlockSpec(memory_space=pl.ANY)
VMEM_LIMIT = 60 * 1024 * 1024


def fsdp_move(value, y=0, z=0, core=0):
    perm = [(i, i ^ (y * 8 + z * 2 + core)) for i in range(32)]
    return lax.ppermute(value, "fsdp", perm)


def dp_move(value, x=0, low=0):
    perm = [(i, i ^ (low * 4 + x)) for i in range(8)]
    return lax.ppermute(value, "dp", perm)


def params(micros):
    return dict(
        cost_estimate=pl.CostEstimate(flops=0, bytes_accessed=int(micros * 3.6e6), transcendentals=0),
    )


def compiler():
    return pltpu.CompilerParams(vmem_limit_bytes=VMEM_LIMIT)


def shifted(near, by, count):
    if by != 0:
        near = pltpu.roll(near, (-by) % near.shape[0], 0)
    return near[PAD : PAD + count]


def sds(shape, dtype):
    return jax.ShapeDtypeStruct(shape, dtype)


def whole(shape):
    return pl.BlockSpec(shape, lambda *_: (0,) * len(shape))


def forward_kernel(lens, par, glu, swished, normed, rstds, masked, *, rows, frames, chunk, unroll):
    step = pl.program_id(0)
    length = lens[0]
    width = glu.shape[1]

    @pl.when(step == 0)
    def _():
        masked[pl.ds(0, PAD), :] = jnp.zeros((PAD, width), F32)
        masked[pl.ds(PAD + frames, PAD), :] = jnp.zeros((PAD, width), F32)

        def fill(i, _):
            at = pl.multiple_of(i * 16, 16)
            ids = at + lax.broadcasted_iota(jnp.int32, (16, 1), 0)
            v = glu[pl.ds(at, 16), :].astype(F32)
            masked[pl.ds(pl.multiple_of(at + PAD, 8), 16), :] = jnp.where(ids < length, v, 0.0)
            return 0

        lax.fori_loop(0, frames // 16, fill, 0, unroll=4)

    def one(i, _):
        local = pl.multiple_of(i * chunk, chunk)
        base = step * rows + local
        near = masked[pl.ds(pl.multiple_of(base, 8), chunk + 2 * PAD), :]
        conv = par[0:1, :] * shifted(near, -2, chunk)
        for k in range(1, TAPS):
            conv = conv + par[k : k + 1, :] * shifted(near, k - 2, chunk)
        mean = jnp.sum(conv, axis=1, keepdims=True) * (1.0 / width)
        cent = conv - mean
        var = jnp.sum(cent * cent, axis=1, keepdims=True) * (1.0 / width)
        rstd = lax.rsqrt(var + 1e-05)
        norm = cent * rstd
        pre = norm * par[5:6, :] + par[6:7, :]
        sig = 0.5 * jnp.tanh(0.5 * pre) + 0.5
        ids = base + lax.broadcasted_iota(jnp.int32, (chunk, 1), 0)
        out = jnp.where(ids < length, pre * sig, 0.0)
        swished[pl.ds(local, chunk), :] = out.astype(BF16)
        normed[pl.ds(local, chunk), :] = norm
        rstds[pl.ds(local, chunk), :] = jnp.broadcast_to(rstd, (chunk, 128))
        return 0

    lax.fori_loop(0, rows // chunk, one, 0, unroll=unroll)


def forward(lens, par, glu, rows=128, chunk=16, unroll=8):
    frames, width = glu.shape
    block = lambda w: pl.BlockSpec((rows, w), lambda i, *_: (i, 0))
    return pl.pallas_call(
        functools.partial(forward_kernel, rows=rows, frames=frames, chunk=chunk, unroll=unroll),
        out_shape=(sds((frames, width), BF16), sds((frames, width), F32), sds((frames, 128), F32)),
        grid_spec=pltpu.PrefetchScalarGridSpec(
            num_scalar_prefetch=1,
            grid=(frames // rows,),
            in_specs=[whole((8, width)), whole((frames, width))],
            out_specs=(block(width), block(width), block(128)),
            scratch_shapes=[pltpu.VMEM((frames + 2 * PAD, width), F32)],
        ),
        compiler_params=compiler(),
        name="forward",
        **params(0.1),
    )(lens, par, glu)


def outer_kernel(core, sw, cot, h1, h2, h3, keep, send):
    res = lax.dot_general(
        sw[...], cot[...], (((0,), (0,)), ((), ())), preferred_element_type=F32
    )
    first = core[0] == 0
    for j in range(4):
        a = res[j * 96 : j * 96 + 48]
        b = res[j * 96 + 48 : j * 96 + 96]
        keep[j] = jnp.where(first, a, b)
        send[j] = jnp.where(first, b, a).astype(BF16)


def outer(core, sw, cot, held):
    frames, width = sw.shape
    return pl.pallas_call(
        outer_kernel,
        out_shape=(sds((16, 48, width), F32), sds((16, 48, width), BF16)),
        grid_spec=pltpu.PrefetchScalarGridSpec(
            num_scalar_prefetch=1,
            grid=(4,),
            in_specs=[
                pl.BlockSpec((frames, 384), lambda i, *_: (0, i)),
                whole((frames, width)),
                HBM,
                HBM,
                HBM,
            ],
            out_specs=(
                pl.BlockSpec((4, 48, width), lambda i, *_: (i, 0, 0)),
                pl.BlockSpec((4, 48, width), lambda i, *_: (i, 0, 0)),
            ),
        ),
        compiler_params=compiler(),
        name="outer",
        **params(0.1),
    )(core, sw, cot, *held)


def stage1_kernel(pos, keep, recv, a0, a1, a2, a3):
    j = pl.program_id(0)
    for n, out in enumerate((a0, a1, a2, a3)):

        @pl.when(j == n)
        def _(out=out):
            out[...] = (keep[0] + recv[0].astype(F32)).astype(out.dtype)


def stage1(pos, keep, recv):
    width = keep.shape[-1]
    keep = keep.reshape(4, 4, 48, width)
    recv = recv.reshape(4, 4, 48, width)
    src = pl.BlockSpec((1, 4, 48, width), lambda j, pos: (pos[0] ^ j, 0, 0, 0))
    return pl.pallas_call(
        stage1_kernel,
        out_shape=tuple(sds((4, 48, width), t) for t in (F32, BF16, BF16, BF16)),
        grid_spec=pltpu.PrefetchScalarGridSpec(
            num_scalar_prefetch=1,
            grid=(4,),
            in_specs=[src, src],
            out_specs=(whole((4, 48, width)),) * 4,
        ),
        compiler_params=compiler(),
        name="stage1",
        **params(0.1),
    )(pos, keep, recv)


def stage2_kernel(pos, a0, a1, a2, a3, held, o0, o1, o2, o3):
    j = pl.program_id(0)
    for n, out in enumerate((o0, o1, o2, o3)):

        @pl.when(j == n)
        def _(out=out):
            total = (a0[0] + a1[0].astype(F32)) + (a2[0].astype(F32) + a3[0].astype(F32))
            out[...] = total.astype(out.dtype)


def stage2(pos, a, held):
    width = a[0].shape[-1]
    src = pl.BlockSpec((1, 48, width), lambda j, pos: (pos[2] ^ j, 0, 0))
    return pl.pallas_call(
        stage2_kernel,
        out_shape=tuple(sds((48, width), t) for t in (F32, BF16, BF16, BF16)),
        grid_spec=pltpu.PrefetchScalarGridSpec(
            num_scalar_prefetch=1,
            grid=(4,),
            in_specs=[src] * 4 + [HBM],
            out_specs=(whole((48, width)),) * 4,
        ),
        compiler_params=compiler(),
        name="stage2",
        **params(3),
    )(pos, *a, held)


def stage3_kernel(pos, v0, v1, v2, v3, h1, h2, o0, o1, o2, o3, total):
    total[...] = (v0[...] + v1[...].astype(F32)) + (v2[...].astype(F32) + v3[...].astype(F32))
    for n, out in enumerate((o0, o1, o2, o3)):
        at = pl.multiple_of((pos[1] ^ n) * 384, 128)
        out[...] = total[:, pl.ds(at, 384)]


def stage3(pos, v, held):
    shape = v[0].shape
    part = (shape[0], 384)
    return pl.pallas_call(
        stage3_kernel,
        out_shape=(sds(part, F32),) * 4,
        grid_spec=pltpu.PrefetchScalarGridSpec(
            num_scalar_prefetch=1,
            grid=(1,),
            in_specs=[whole(shape)] * 4 + [HBM] * 2,
            out_specs=(whole(part),) * 4,
            scratch_shapes=[pltpu.VMEM(shape, F32)],
        ),
        compiler_params=compiler(),
        name="stage3",
        **params(2),
    )(pos, *v, *held)


def pack_kernel(v0, v1, v2, v3, small, out):
    out[0:48, :] = (v0[...] + v1[...]) + (v2[...] + v3[...])
    out[48:56, :] = small[...]


def pack(v, small):
    rows, width = v[0].shape
    return pl.pallas_call(
        pack_kernel,
        out_shape=sds((rows + 8, width), F32),
        grid=(1,),
        in_specs=[whole((rows, width))] * 4 + [whole((8, width))],
        out_specs=whole((rows + 8, width)),
        compiler_params=compiler(),
        name="pack",
        **params(1),
    )(*v, small)


def join_kernel(pos, v0, v1, v2, v3, out, small):
    for n, v in enumerate((v0, v1, v2, v3)):
        at = pl.multiple_of((pos[1] ^ n) * 384, 128)
        out[:, pl.ds(at, 384)] = v[0:48, :]
    small[...] = (v0[48:56, :] + v1[48:56, :]) + (v2[48:56, :] + v3[48:56, :])


def join(pos, parts):
    rows = parts[0].shape[0] - 8
    return pl.pallas_call(
        join_kernel,
        out_shape=(sds((rows, 1536), F32), sds((8, 384), F32)),
        grid_spec=pltpu.PrefetchScalarGridSpec(
            num_scalar_prefetch=1,
            grid=(1,),
            in_specs=[whole((rows + 8, 384))] * 4,
            out_specs=(whole((rows, 1536)), whole((8, 384))),
        ),
        compiler_params=compiler(),
        name="join",
        **params(2),
    )(pos, *parts)


def gather_kernel(w0, w1, w2, w3, held, out):
    rows = w0.shape[0]
    for n, w in enumerate((w0, w1, w2, w3)):
        out[n * rows : n * rows + rows, :] = w[...]


def gather(w, held):
    rows, width = w[0].shape
    return pl.pallas_call(
        gather_kernel,
        out_shape=sds((4 * rows, width), BF16),
        grid=(1,),
        in_specs=[whole((rows, width))] * 4 + [HBM],
        out_specs=whole((4 * rows, width)),
        compiler_params=compiler(),
        name="gather",
        **params(0.1),
    )(*w, held)


def fetch_weight(pos, pieces, buf, sem):
    y, z, core = pos[0], pos[2], pos[3]
    copies = []
    for n, piece in enumerate(pieces):
        dc, dy = n // 4, n % 4
        for dz in range(4):
            index = ((y ^ dy) * 4 + (z ^ dz)) * 2 + (core ^ dc)
            at = pl.multiple_of(index * 48, 48)
            copies.append(
                pltpu.make_async_copy(
                    piece.at[pl.ds(dz * 48, 48), :], buf.at[pl.ds(at, 48), :], sem.at[n * 4 + dz]
                )
            )
    for c in copies:
        c.start()
    for c in copies:
        c.wait()


def project_kernel(pos, *refs):
    pieces, (sw, res, _, _, out, buf, sem) = refs[:8], refs[8:]

    @pl.when(pl.program_id(0) == 0)
    def _():
        fetch_weight(pos, pieces, buf, sem)

    prod = jnp.dot(sw[...], buf[...], preferred_element_type=F32)
    out[...] = (res[...].astype(F32) + prod).astype(BF16)


def project(pos, pieces, sw, res, held, rows=256):
    frames, width = sw.shape
    block = pl.BlockSpec((rows, width), lambda i, *_: (i, 0))
    return pl.pallas_call(
        project_kernel,
        out_shape=sds((frames, width), BF16),
        grid_spec=pltpu.PrefetchScalarGridSpec(
            num_scalar_prefetch=1,
            grid=(frames // rows,),
            in_specs=[HBM] * 8 + [block, block, HBM, HBM],
            out_specs=block,
            scratch_shapes=[pltpu.VMEM((width, width), BF16), pltpu.SemaphoreType.DMA((32,))],
        ),
        compiler_params=compiler(),
        name="project",
        **params(11),
    )(pos, *pieces, sw, res, *held)


def backward_kernel(pos, *refs, rows, chunk, unroll):
    pieces = refs[:8]
    par, cot, nrm, rst, _, gconv, sums, buf, sem, grad = refs[8:]
    step = pl.program_id(0)
    width = cot.shape[1]
    length = pos[4]

    @pl.when(step == 0)
    def _():
        fetch_weight(pos, pieces, buf, sem)
        sums[...] = jnp.zeros_like(sums)

    grad[...] = lax.dot_general(
        cot[...], buf[...], (((1,), (1,)), ((), ())), preferred_element_type=F32
    )

    def one(i, _):
        at = pl.multiple_of(i * chunk, chunk)
        gain = par[5:6, :]
        norm = nrm[pl.ds(at, chunk), :]
        pre = norm * gain + par[6:7, :]
        sig = 0.5 * jnp.tanh(0.5 * pre) + 0.5
        ids = step * rows + at + lax.broadcasted_iota(jnp.int32, (chunk, 1), 0)
        gs = jnp.where(ids < length, grad[pl.ds(at, chunk), :], 0.0)
        gpre = gs * (sig * (1.0 + pre * (1.0 - sig)))
        gn = gpre * norm
        for h in range(chunk // 8):
            sums[0] += gn[h * 8 : h * 8 + 8]
            sums[1] += gpre[h * 8 : h * 8 + 8]
        gnorm = gpre * gain
        m1 = jnp.sum(gnorm, axis=1, keepdims=True) * (1.0 / width)
        m2 = jnp.sum(gnorm * norm, axis=1, keepdims=True) * (1.0 / width)
        gconv[pl.ds(at, chunk), :] = rst[pl.ds(at, chunk), 0:1] * (gnorm - m1 - norm * m2)
        return 0

    lax.fori_loop(0, rows // chunk, one, 0, unroll=unroll)


def backward(pos, pieces, par, cot, nrm, rst, held, rows=256, chunk=16, unroll=4):
    frames, width = cot.shape
    block = lambda w: pl.BlockSpec((rows, w), lambda i, *_: (i, 0))
    return pl.pallas_call(
        functools.partial(backward_kernel, rows=rows, chunk=chunk, unroll=unroll),
        out_shape=(sds((frames, width), F32), sds((2, 8, width), F32)),
        grid_spec=pltpu.PrefetchScalarGridSpec(
            num_scalar_prefetch=1,
            grid=(frames // rows,),
            in_specs=[HBM] * 8
            + [whole((8, width)), block(width), block(width), block(128), HBM],
            out_specs=(block(width), whole((2, 8, width))),
            scratch_shapes=[
                pltpu.VMEM((width, width), BF16),
                pltpu.SemaphoreType.DMA((32,)),
                pltpu.VMEM((rows, width), F32),
            ],
        ),
        compiler_params=compiler(),
        name="backward",
        **params(0.1),
    )(pos, *pieces, par, cot, nrm, rst, held)


def taps_kernel(pos, par, glu, gconv, norm_sums, out, small, pad, sums, *, rows, frames, chunk, unroll, strip):
    step = pl.program_id(0)
    width = glu.shape[1]
    length = pos[4]

    @pl.when(step == 0)
    def _():
        sums[...] = jnp.zeros_like(sums)
        pad[pl.ds(0, PAD), :] = jnp.zeros((PAD, width), F32)
        pad[pl.ds(PAD + frames, PAD), :] = jnp.zeros((PAD, width), F32)

    @pl.when(step < frames // rows)
    def _():
        pad[pl.ds(pl.multiple_of(PAD + step * rows, 8), rows), :] = gconv[...]

    @pl.when(step > 0)
    def _():
        start = (step - 1) * rows
        for c in range(0, width, strip):
            cols = slice(c, c + strip)

            def one(i, acc, cols=cols):
                at = pl.multiple_of(i * chunk, chunk)
                base = pl.multiple_of(start + at, 8)
                live = base + lax.broadcasted_iota(jnp.int32, (chunk, 1), 0) < length
                mk = jnp.where(live, glu[pl.ds(at, chunk), cols].astype(F32), 0.0)
                near = pad[pl.ds(base, chunk + 2 * PAD), cols]
                grad, new = None, []
                for k in range(TAPS):
                    g = shifted(near, 2 - k, chunk)
                    term = par[k : k + 1, cols] * g
                    grad = term if grad is None else grad + term
                    p = mk * g
                    new.append(acc[k] + sum(p[h : h + 8] for h in range(0, chunk, 8)))
                out[pl.ds(at, chunk), cols] = jnp.where(live, grad, 0.0).astype(BF16)
                return tuple(new)

            zero = jnp.zeros((8, strip), F32)
            acc = lax.fori_loop(0, rows // chunk, one, (zero,) * TAPS, unroll=unroll)
            for k in range(TAPS):
                sums[k, :, cols] += acc[k]

    @pl.when(step == frames // rows)
    def _():
        for k in range(TAPS):
            small[k : k + 1, :] = jnp.sum(sums[k], axis=0, keepdims=True)
        for k in range(2):
            small[TAPS + k : TAPS + k + 1, :] = jnp.sum(norm_sums[k], axis=0, keepdims=True)
        small[TAPS + 2 :, :] = jnp.zeros((1, width), F32)


def taps(pos, par, glu, gconv, norm_sums, rows=128, chunk=32, unroll=2, strip=256):
    frames, width = glu.shape
    last = frames // rows - 1
    late = pl.BlockSpec((rows, width), lambda i, *_: (jnp.maximum(i - 1, 0), 0))
    return pl.pallas_call(
        functools.partial(taps_kernel, rows=rows, frames=frames, chunk=chunk, unroll=unroll, strip=strip),
        out_shape=(sds((frames, width), BF16), sds((8, width), F32)),
        grid_spec=pltpu.PrefetchScalarGridSpec(
            num_scalar_prefetch=1,
            grid=(frames // rows + 1,),
            in_specs=[
                whole((8, width)),
                late,
                pl.BlockSpec((rows, width), lambda i, *_: (jnp.minimum(i, last), 0)),
                whole((2, 8, width)),
            ],
            out_specs=(late, whole((8, width))),
            scratch_shapes=[pltpu.VMEM((frames + 2 * PAD, width), F32), pltpu.VMEM((TAPS, 8, width), F32)],
        ),
        compiler_params=compiler(),
        name="taps",
        **params(0.1),
    )(pos, par, glu, gconv, norm_sums)


def local(glu_out, residual_in, cotangent, lengths, conv_kernel, norm_gain, norm_bias, proj_weight):
    _, frames, width = glu_out.shape
    glu, res, cot = glu_out[0], residual_in[0], cotangent[0]
    f, d = lax.axis_index("fsdp"), lax.axis_index("dp")
    core, z, y = f % 2, (f // 2) % 4, f // 8
    x = d % 4
    pos = jnp.stack([y, x, z, core, lengths[0]]).astype(jnp.int32)

    own = jnp.concatenate([conv_kernel, norm_gain[None], norm_bias[None]], axis=0)
    own = jnp.pad(own, ((0, 1), (0, 0)))
    par = lax.dynamic_update_slice(jnp.zeros((8, width), BF16), own, (0, f * 48))
    par = par + fsdp_move(par, core=1)
    par = (par + fsdp_move(par, y=1)) + (fsdp_move(par, y=2) + fsdp_move(par, y=3))
    par = par + fsdp_move(par, z=1)
    par = par + fsdp_move(par, z=3)
    par = par.astype(F32)

    block = gather([proj_weight] + [fsdp_move(proj_weight, z=k) for k in (1, 2, 3)], own)
    near = [block] + [fsdp_move(block, y=k) for k in (1, 2, 3)]
    pieces = near + [fsdp_move(p, core=1) for p in near]

    swished, normed, rstd = forward(lengths, par, glu)
    keep, send = outer(core[None].astype(jnp.int32), swished, cot, near[1:])
    recv = fsdp_move(send, core=1)
    a = stage1(pos, keep, recv)
    gconv, sums = backward(pos, pieces, par, cot, normed, rstd, a[0])
    glu_grad, small = taps(pos, par, glu, gconv, sums)
    v = stage2(pos, [a[0]] + [fsdp_move(a[k], y=k) for k in (1, 2, 3)], glu_grad)
    small = small + fsdp_move(small, core=1)
    small = (small + fsdp_move(small, y=1)) + (fsdp_move(small, y=2) + fsdp_move(small, y=3))
    block_out = project(pos, pieces, swished, res, (v[0], small))
    small = small + fsdp_move(small, z=1)
    v = stage3(pos, [v[0]] + [fsdp_move(v[k], z=k) for k in (1, 2, 3)], (block_out, small))
    small = small + fsdp_move(small, z=3)
    small = jnp.pad(lax.dynamic_slice(small, (0, f * 48), (8, 48)), ((0, 0), (0, 336)))
    total = pack([v[0]] + [dp_move(v[k], x=k) for k in (1, 2, 3)], small)
    total = total + dp_move(total, low=1)
    proj_grad, small = join(pos, [total] + [dp_move(total, x=k) for k in (1, 2, 3)])
    return (block_out[None], glu_grad[None], proj_grad, small[:TAPS, :48], small[TAPS : TAPS + 2, :48])


def solution(mesh):
    rows = P(("dp", "fsdp"), None, None)
    return jax.shard_map(
        local,
        mesh=mesh,
        in_specs=(rows, rows, rows, P(("dp", "fsdp")), P(None, "fsdp"), P("fsdp"), P("fsdp"), P("fsdp", None)),
        out_specs=(rows, rows, P("fsdp", None), P(None, "fsdp"), P(None, "fsdp")),
        check_vma=False,
    )
```

```python
import functools

import jax
import jax.numpy as jnp
from jax import lax
from jax.experimental import pallas as pl
from jax.experimental.pallas import tpu as pltpu
from jax.sharding import PartitionSpec as P

TAPS = 5
NX, NY, NZ = 4, 4, 4
F32, BF16 = jnp.float32, jnp.bfloat16
PAD = 8
HBM = pl.BlockSpec(memory_space=pl.ANY)
VMEM_LIMIT = 60 * 1024 * 1024


def fsdp_move(value, y=0, z=0, core=0):
    perm = [(i, i ^ (y * 8 + z * 2 + core)) for i in range(32)]
    return lax.ppermute(value, "fsdp", perm)


def dp_move(value, x=0, low=0):
    perm = [(i, i ^ (low * 4 + x)) for i in range(8)]
    return lax.ppermute(value, "dp", perm)


def params(micros):
    return dict(
        cost_estimate=pl.CostEstimate(flops=0, bytes_accessed=int(micros * 3.6e6), transcendentals=0),
    )


def compiler():
    return pltpu.CompilerParams(vmem_limit_bytes=VMEM_LIMIT)


def shifted(near, by, count):
    if by != 0:
        near = pltpu.roll(near, (-by) % near.shape[0], 0)
    return near[PAD : PAD + count]


def sds(shape, dtype):
    return jax.ShapeDtypeStruct(shape, dtype)


def whole(shape):
    return pl.BlockSpec(shape, lambda *_: (0,) * len(shape))


def forward_kernel(lens, par, glu, swished, normed, rstds, masked, *, rows, frames, chunk, unroll):
    step = pl.program_id(0)
    length = lens[0]
    width = glu.shape[1]

    @pl.when(step == 0)
    def _():
        masked[pl.ds(0, PAD), :] = jnp.zeros((PAD, width), F32)
        masked[pl.ds(PAD + frames, PAD), :] = jnp.zeros((PAD, width), F32)

        def fill(i, _):
            at = pl.multiple_of(i * 16, 16)
            ids = at + lax.broadcasted_iota(jnp.int32, (16, 1), 0)
            v = glu[pl.ds(at, 16), :].astype(F32)
            masked[pl.ds(pl.multiple_of(at + PAD, 8), 16), :] = jnp.where(ids < length, v, 0.0)
            return 0

        lax.fori_loop(0, frames // 16, fill, 0, unroll=4)

    def one(i, _):
        local = pl.multiple_of(i * chunk, chunk)
        base = step * rows + local
        near = masked[pl.ds(pl.multiple_of(base, 8), chunk + 2 * PAD), :]
        conv = par[0:1, :] * shifted(near, -2, chunk)
        for k in range(1, TAPS):
            conv = conv + par[k : k + 1, :] * shifted(near, k - 2, chunk)
        mean = jnp.sum(conv, axis=1, keepdims=True) * (1.0 / width)
        cent = conv - mean
        var = jnp.sum(cent * cent, axis=1, keepdims=True) * (1.0 / width)
        rstd = lax.rsqrt(var + 1e-05)
        norm = cent * rstd
        pre = norm * par[5:6, :] + par[6:7, :]
        sig = 0.5 * jnp.tanh(0.5 * pre) + 0.5
        ids = base + lax.broadcasted_iota(jnp.int32, (chunk, 1), 0)
        out = jnp.where(ids < length, pre * sig, 0.0)
        swished[pl.ds(local, chunk), :] = out.astype(BF16)
        normed[pl.ds(local, chunk), :] = norm
        rstds[pl.ds(local, chunk), :] = jnp.broadcast_to(rstd, (chunk, 128))
        return 0

    lax.fori_loop(0, rows // chunk, one, 0, unroll=unroll)


def forward(lens, par, glu, rows=128, chunk=16, unroll=8):
    frames, width = glu.shape
    block = lambda w: pl.BlockSpec((rows, w), lambda i, *_: (i, 0))
    return pl.pallas_call(
        functools.partial(forward_kernel, rows=rows, frames=frames, chunk=chunk, unroll=unroll),
        out_shape=(sds((frames, width), BF16), sds((frames, width), F32), sds((frames, 128), F32)),
        grid_spec=pltpu.PrefetchScalarGridSpec(
            num_scalar_prefetch=1,
            grid=(frames // rows,),
            in_specs=[whole((8, width)), whole((frames, width))],
            out_specs=(block(width), block(width), block(128)),
            scratch_shapes=[pltpu.VMEM((frames + 2 * PAD, width), F32)],
        ),
        compiler_params=compiler(),
        name="forward",
        **params(0.1),
    )(lens, par, glu)


def outer_kernel(core, sw, cot, h1, h2, keep, send):
    res = lax.dot_general(
        sw[...], cot[...], (((0,), (0,)), ((), ())), preferred_element_type=F32
    )
    first = core[0] == 0
    for j in range(4):
        a = res[j * 96 : j * 96 + 48]
        b = res[j * 96 + 48 : j * 96 + 96]
        keep[j] = jnp.where(first, a, b)
        send[j] = jnp.where(first, b, a).astype(BF16)


def outer(core, sw, cot, held):
    frames, width = sw.shape
    return pl.pallas_call(
        outer_kernel,
        out_shape=(sds((16, 48, width), F32), sds((16, 48, width), BF16)),
        grid_spec=pltpu.PrefetchScalarGridSpec(
            num_scalar_prefetch=1,
            grid=(4,),
            in_specs=[
                pl.BlockSpec((frames, 384), lambda i, *_: (0, i)),
                whole((frames, width)),
                HBM,
                HBM,
            ],
            out_specs=(
                pl.BlockSpec((4, 48, width), lambda i, *_: (i, 0, 0)),
                pl.BlockSpec((4, 48, width), lambda i, *_: (i, 0, 0)),
            ),
        ),
        compiler_params=compiler(),
        name="outer",
        **params(0.1),
    )(core, sw, cot, *held)


def stage1_kernel(pos, keep, recv, a0, a1, a2, a3):
    j = pl.program_id(0)
    for n, out in enumerate((a0, a1, a2, a3)):

        @pl.when(j == n)
        def _(out=out):
            out[...] = (keep[0] + recv[0].astype(F32)).astype(out.dtype)


def stage1(pos, keep, recv):
    width = keep.shape[-1]
    keep = keep.reshape(4, 4, 48, width)
    recv = recv.reshape(4, 4, 48, width)
    src = pl.BlockSpec((1, 4, 48, width), lambda j, pos: (pos[0] ^ j, 0, 0, 0))
    return pl.pallas_call(
        stage1_kernel,
        out_shape=tuple(sds((4, 48, width), t) for t in (F32, BF16, BF16, BF16)),
        grid_spec=pltpu.PrefetchScalarGridSpec(
            num_scalar_prefetch=1,
            grid=(4,),
            in_specs=[src, src],
            out_specs=(whole((4, 48, width)),) * 4,
        ),
        compiler_params=compiler(),
        name="stage1",
        **params(0.1),
    )(pos, keep, recv)


def stage2_kernel(pos, a0, a1, a2, a3, held, o0, o1, o2, o3):
    j = pl.program_id(0)
    for n, out in enumerate((o0, o1, o2, o3)):

        @pl.when(j == n)
        def _(out=out):
            total = (a0[0] + a1[0].astype(F32)) + (a2[0].astype(F32) + a3[0].astype(F32))
            out[...] = total.astype(out.dtype)


def stage2(pos, a, held):
    width = a[0].shape[-1]
    src = pl.BlockSpec((1, 48, width), lambda j, pos: (pos[2] ^ j, 0, 0))
    return pl.pallas_call(
        stage2_kernel,
        out_shape=tuple(sds((48, width), t) for t in (F32, BF16, BF16, BF16)),
        grid_spec=pltpu.PrefetchScalarGridSpec(
            num_scalar_prefetch=1,
            grid=(4,),
            in_specs=[src] * 4 + [HBM],
            out_specs=(whole((48, width)),) * 4,
        ),
        compiler_params=compiler(),
        name="stage2",
        **params(3),
    )(pos, *a, held)


def stage3_kernel(pos, v0, v1, v2, v3, held, o0, o1, o2, o3, total):
    total[...] = (v0[...] + v1[...].astype(F32)) + (v2[...].astype(F32) + v3[...].astype(F32))
    for n, out in enumerate((o0, o1, o2, o3)):
        at = pl.multiple_of((pos[1] ^ n) * 384, 128)
        out[...] = total[:, pl.ds(at, 384)]


def stage3(pos, v, held):
    shape = v[0].shape
    part = (shape[0], 384)
    return pl.pallas_call(
        stage3_kernel,
        out_shape=(sds(part, F32),) * 4,
        grid_spec=pltpu.PrefetchScalarGridSpec(
            num_scalar_prefetch=1,
            grid=(1,),
            in_specs=[whole(shape)] * 4 + [HBM],
            out_specs=(whole(part),) * 4,
            scratch_shapes=[pltpu.VMEM(shape, F32)],
        ),
        compiler_params=compiler(),
        name="stage3",
        **params(2),
    )(pos, *v, held)


def join_kernel(pos, v0, v1, v2, v3, out):
    for n, v in enumerate((v0, v1, v2, v3)):
        at = pl.multiple_of((pos[1] ^ n) * 384, 128)
        out[:, pl.ds(at, 384)] = v[...]


def join(pos, parts):
    rows = parts[0].shape[0]
    return pl.pallas_call(
        join_kernel,
        out_shape=sds((rows, 1536), F32),
        grid_spec=pltpu.PrefetchScalarGridSpec(
            num_scalar_prefetch=1,
            grid=(1,),
            in_specs=[whole((rows, 384))] * 4,
            out_specs=whole((rows, 1536)),
        ),
        compiler_params=compiler(),
        name="join",
        **params(2),
    )(pos, *parts)


def gather_kernel(*refs):
    parts, out = refs[:-2], refs[-1]
    rows = parts[0].shape[0]
    for n, w in enumerate(parts):
        out[n * rows : n * rows + rows, :] = w[...]


def gather(w, held):
    rows, width = w[0].shape
    return pl.pallas_call(
        gather_kernel,
        out_shape=sds((len(w) * rows, width), BF16),
        grid=(1,),
        in_specs=[whole((rows, width))] * len(w) + [HBM],
        out_specs=whole((len(w) * rows, width)),
        compiler_params=compiler(),
        name="gather",
        **params(0.1),
    )(*w, held)


def fetch_weight(pos, pieces, buf, sem):
    y, z, core = pos[0], pos[2], pos[3]
    copies = []
    for n, piece in enumerate(pieces):
        dc, dy = n // 4, n % 4
        for dz in range(4):
            index = ((y ^ dy) * 4 + (z ^ dz)) * 2 + (core ^ dc)
            at = pl.multiple_of(index * 48, 48)
            copies.append(
                pltpu.make_async_copy(
                    piece.at[pl.ds(dz * 48, 48), :], buf.at[pl.ds(at, 48), :], sem.at[n * 4 + dz]
                )
            )
    for c in copies:
        c.start()
    for c in copies:
        c.wait()


def project_kernel(pos, *refs):
    pieces, (sw, res, _, _, out, buf, sem) = refs[:8], refs[8:]

    @pl.when(pl.program_id(0) == 0)
    def _():
        fetch_weight(pos, pieces, buf, sem)

    prod = jnp.dot(sw[...], buf[...], preferred_element_type=F32)
    out[...] = (res[...].astype(F32) + prod).astype(BF16)


def project(pos, pieces, sw, res, held, rows=256):
    frames, width = sw.shape
    block = pl.BlockSpec((rows, width), lambda i, *_: (i, 0))
    return pl.pallas_call(
        project_kernel,
        out_shape=sds((frames, width), BF16),
        grid_spec=pltpu.PrefetchScalarGridSpec(
            num_scalar_prefetch=1,
            grid=(frames // rows,),
            in_specs=[HBM] * 8 + [block, block, HBM, HBM],
            out_specs=block,
            scratch_shapes=[pltpu.VMEM((width, width), BF16), pltpu.SemaphoreType.DMA((32,))],
        ),
        compiler_params=compiler(),
        name="project",
        **params(11),
    )(pos, *pieces, sw, res, *held)


def backward_kernel(pos, *refs, rows, chunk, unroll):
    pieces = refs[:8]
    par, cot, nrm, rst, _, gconv, sums, buf, sem, grad = refs[8:]
    step = pl.program_id(0)
    width = cot.shape[1]
    length = pos[4]

    @pl.when(step == 0)
    def _():
        fetch_weight(pos, pieces, buf, sem)
        sums[...] = jnp.zeros_like(sums)

    grad[...] = lax.dot_general(
        cot[...], buf[...], (((1,), (1,)), ((), ())), preferred_element_type=F32
    )

    def one(i, _):
        at = pl.multiple_of(i * chunk, chunk)
        gain = par[5:6, :]
        norm = nrm[pl.ds(at, chunk), :]
        pre = norm * gain + par[6:7, :]
        sig = 0.5 * jnp.tanh(0.5 * pre) + 0.5
        ids = step * rows + at + lax.broadcasted_iota(jnp.int32, (chunk, 1), 0)
        gs = jnp.where(ids < length, grad[pl.ds(at, chunk), :], 0.0)
        gpre = gs * (sig * (1.0 + pre * (1.0 - sig)))
        gn = gpre * norm
        for h in range(chunk // 8):
            sums[0] += gn[h * 8 : h * 8 + 8]
            sums[1] += gpre[h * 8 : h * 8 + 8]
        gnorm = gpre * gain
        m1 = jnp.sum(gnorm, axis=1, keepdims=True) * (1.0 / width)
        m2 = jnp.sum(gnorm * norm, axis=1, keepdims=True) * (1.0 / width)
        gconv[pl.ds(at, chunk), :] = rst[pl.ds(at, chunk), 0:1] * (gnorm - m1 - norm * m2)
        return 0

    lax.fori_loop(0, rows // chunk, one, 0, unroll=unroll)


def backward(pos, pieces, par, cot, nrm, rst, held, rows=256, chunk=16, unroll=4):
    frames, width = cot.shape
    block = lambda w: pl.BlockSpec((rows, w), lambda i, *_: (i, 0))
    return pl.pallas_call(
        functools.partial(backward_kernel, rows=rows, chunk=chunk, unroll=unroll),
        out_shape=(sds((frames, width), F32), sds((2, 8, width), F32)),
        grid_spec=pltpu.PrefetchScalarGridSpec(
            num_scalar_prefetch=1,
            grid=(frames // rows,),
            in_specs=[HBM] * 8
            + [whole((8, width)), block(width), block(width), block(128), HBM],
            out_specs=(block(width), whole((2, 8, width))),
            scratch_shapes=[
                pltpu.VMEM((width, width), BF16),
                pltpu.SemaphoreType.DMA((32,)),
                pltpu.VMEM((rows, width), F32),
            ],
        ),
        compiler_params=compiler(),
        name="backward",
        **params(0.1),
    )(pos, *pieces, par, cot, nrm, rst, held)


def taps_kernel(pos, par, glu, gconv, norm_sums, out, small, pad, sums, *, rows, frames, chunk, unroll, strip):
    step = pl.program_id(0)
    width = glu.shape[1]
    length = pos[4]

    @pl.when(step == 0)
    def _():
        sums[...] = jnp.zeros_like(sums)
        pad[pl.ds(0, PAD), :] = jnp.zeros((PAD, width), F32)
        pad[pl.ds(PAD + frames, PAD), :] = jnp.zeros((PAD, width), F32)

    @pl.when(step < frames // rows)
    def _():
        pad[pl.ds(pl.multiple_of(PAD + step * rows, 8), rows), :] = gconv[...]

    @pl.when(step > 0)
    def _():
        start = (step - 1) * rows
        for c in range(0, width, strip):
            cols = slice(c, c + strip)

            def one(i, acc, cols=cols):
                at = pl.multiple_of(i * chunk, chunk)
                base = pl.multiple_of(start + at, 8)
                live = base + lax.broadcasted_iota(jnp.int32, (chunk, 1), 0) < length
                mk = jnp.where(live, glu[pl.ds(at, chunk), cols].astype(F32), 0.0)
                near = pad[pl.ds(base, chunk + 2 * PAD), cols]
                grad, new = None, []
                for k in range(TAPS):
                    g = shifted(near, 2 - k, chunk)
                    term = par[k : k + 1, cols] * g
                    grad = term if grad is None else grad + term
                    p = mk * g
                    new.append(acc[k] + sum(p[h : h + 8] for h in range(0, chunk, 8)))
                out[pl.ds(at, chunk), cols] = jnp.where(live, grad, 0.0).astype(BF16)
                return tuple(new)

            zero = jnp.zeros((8, strip), F32)
            acc = lax.fori_loop(0, rows // chunk, one, (zero,) * TAPS, unroll=unroll)
            for k in range(TAPS):
                sums[k, :, cols] += acc[k]

    @pl.when(step == frames // rows)
    def _():
        for k in range(TAPS):
            small[k : k + 1, :] = jnp.sum(sums[k], axis=0, keepdims=True)
        for k in range(2):
            small[TAPS + k : TAPS + k + 1, :] = jnp.sum(norm_sums[k], axis=0, keepdims=True)
        small[TAPS + 2 :, :] = jnp.zeros((1, width), F32)


def taps(pos, par, glu, gconv, norm_sums, rows=128, chunk=32, unroll=2, strip=256):
    frames, width = glu.shape
    last = frames // rows - 1
    late = pl.BlockSpec((rows, width), lambda i, *_: (jnp.maximum(i - 1, 0), 0))
    return pl.pallas_call(
        functools.partial(taps_kernel, rows=rows, frames=frames, chunk=chunk, unroll=unroll, strip=strip),
        out_shape=(sds((frames, width), BF16), sds((8, width), F32)),
        grid_spec=pltpu.PrefetchScalarGridSpec(
            num_scalar_prefetch=1,
            grid=(frames // rows + 1,),
            in_specs=[
                whole((8, width)),
                late,
                pl.BlockSpec((rows, width), lambda i, *_: (jnp.minimum(i, last), 0)),
                whole((2, 8, width)),
            ],
            out_specs=(late, whole((8, width))),
            scratch_shapes=[pltpu.VMEM((frames + 2 * PAD, width), F32), pltpu.VMEM((TAPS, 8, width), F32)],
        ),
        compiler_params=compiler(),
        name="taps",
        **params(0.1),
    )(pos, par, glu, gconv, norm_sums)


def local(glu_out, residual_in, cotangent, lengths, conv_kernel, norm_gain, norm_bias, proj_weight):
    _, frames, width = glu_out.shape
    glu, res, cot = glu_out[0], residual_in[0], cotangent[0]
    f, d = lax.axis_index("fsdp"), lax.axis_index("dp")
    core, z, y = f % 2, (f // 2) % 4, f // 8
    x = d % 4
    pos = jnp.stack([y, x, z, core, lengths[0]]).astype(jnp.int32)

    own = jnp.concatenate([conv_kernel, norm_gain[None], norm_bias[None]], axis=0)
    own = jnp.pad(own, ((0, 1), (0, 0)))
    par = lax.dynamic_update_slice(jnp.zeros((8, width), BF16), own, (0, f * 48))
    par = par + fsdp_move(par, core=1)
    par = (par + fsdp_move(par, y=1)) + (fsdp_move(par, y=2) + fsdp_move(par, y=3))
    half = par + fsdp_move(par, z=1)
    par = half + fsdp_move(half, z=3)
    par = par.astype(F32)

    block = gather([proj_weight] + [fsdp_move(proj_weight, z=k) for k in (1, 2, 3)], half)
    near = [block] + [fsdp_move(block, y=k) for k in (1, 2, 3)]

    swished, normed, rstd = forward(lengths, par, glu)
    keep, send = outer(core[None].astype(jnp.int32), swished, cot, (near[1], near[3]))
    recv = fsdp_move(send, core=1)
    a = stage1(pos, keep, recv)
    near[2] = gather(near[2:3], a[0])
    pieces = near + [fsdp_move(p, core=1) for p in near]
    gconv, sums = backward(pos, pieces, par, cot, normed, rstd, a[0])
    glu_grad, small = taps(pos, par, glu, gconv, sums)
    v = stage2(pos, [a[0]] + [fsdp_move(a[k], y=k) for k in (1, 2, 3)], glu_grad)
    small = small + fsdp_move(small, core=1)
    small = (small + fsdp_move(small, y=1)) + (fsdp_move(small, y=2) + fsdp_move(small, y=3))
    block_out = project(pos, pieces, swished, res, (v[0], small))
    v = stage3(pos, [v[0]] + [fsdp_move(v[k], z=k) for k in (1, 2, 3)], block_out)
    total = (v[0] + dp_move(v[1], x=1)) + (dp_move(v[2], x=2) + dp_move(v[3], x=3))
    total = total + dp_move(total, low=1)
    proj_grad = join(pos, [total] + [dp_move(total, x=k) for k in (1, 2, 3)])

    small = small + fsdp_move(small, z=1)
    small = small + fsdp_move(small, z=3)
    small = lax.dynamic_slice(small, (0, f * 48), (8, 48))
    small = (small + dp_move(small, x=1)) + (dp_move(small, x=2) + dp_move(small, x=3))
    small = small + dp_move(small, low=1)
    return (block_out[None], glu_grad[None], proj_grad, small[:TAPS], small[TAPS : TAPS + 2])


def solution(mesh):
    rows = P(("dp", "fsdp"), None, None)
    return jax.shard_map(
        local,
        mesh=mesh,
        in_specs=(rows, rows, rows, P(("dp", "fsdp")), P(None, "fsdp"), P("fsdp"), P("fsdp"), P("fsdp", None)),
        out_specs=(rows, rows, P("fsdp", None), P(None, "fsdp"), P(None, "fsdp")),
        check_vma=False,
    )
```
